128 devices in a mesh: row: 16 (over y, z_lo, core), col: 8 (over x, z_hi).
Axes of the slice: x: 4, y: 4, z: 4 (z_hi: 2, z_lo: 2; z = z_hi * 2 + z_lo), core: 2. Of those that a mesh axis runs over, the one named last changes fastest.
Arguments:
- patches: bfloat16 [128, 128, 1280], P('row', 'col'), may hold values from -6 to 6
- norm_gain: float32 [1280], replicated, may hold values from 0.1 to 1.9
- query_weight: bfloat16 [1280, 1280], P(None, 'col'), may hold values from -12 to 12
- key_weight: bfloat16 [1280, 1280], P(None, 'col'), may hold values from -0.15625 to 0.15625
- value_weight: bfloat16 [1280, 1280], P(None, 'col'), may hold values from -0.15625 to 0.15625
- out_weight: bfloat16 [1280, 1280], replicated, may hold values from -0.15625 to 0.15625
- merge_gain: float32 [1280], replicated, may hold values from 0.1 to 1.9
- up_weight: bfloat16 [5120, 5120], P(None, 'col'), may hold values from -0.078125 to 0.078125
- up_bias: float32 [5120], P('col'), may hold values from -3 to 3
- down_weight: bfloat16 [5120, 8192], P('col'), may hold values from -0.078125 to 0.078125
- down_bias: float32 [8192], replicated, may hold values from -3 to 3
Outputs:
- merged_tokens: bfloat16 [4096, 8192], P(('row', 'col'))
The draws below stay inside these ranges and needn't reach their ends.
All inputs are finite; a program needn't handle non-finite values.
Results may differ from the reference program's by a relative error of at most 0.018.
The reference program's roundings to bfloat16 on the way count: a program that leaves them out, or rounds other values in their place, can miss the bound.
Values may be sent and summed in bfloat16 or wider, within the bound.
No kernel may reach another device: no remote copies, remote signals or barrier semaphores. Data moves between devices by JAX's collectives and lax.ppermute only.
A program may use at most 128 MiB of HBM per device.

```python
import math
import jax
import jax.numpy as jnp
from jax import lax

D = 1280
HEADS = 16
HEAD_DIM = 80
HID = 5120
OUT = 8192
GH = 128
GW = 128
MTOK = 4096
N_COL = 8


def draw_query_weight(key, part):
    normal_draw = jnp.clip(jax.random.normal(key, (D, D), jnp.float32), -6.0, 6.0) * (3.5 / math.sqrt(D))
    return jnp.clip(normal_draw, -12.0, 12.0).astype(jnp.bfloat16)


def block_levels(rng, dims, cuts, least, largest):
    level, own = 1.0, jax.random.fold_in(rng, 6)
    for position, parts in cuts:
        draws = jnp.exp(jax.random.uniform(jax.random.fold_in(own, position), (parts,), jnp.float32, least / len(cuts), largest / len(cuts)))
        level = level * jnp.repeat(draws, dims[position] // parts).reshape([-1 if axis == position else 1 for axis in range(len(dims))])
    return level


def gaussian(own_key, dims, width, bound, split=(), kind=jnp.bfloat16):
    drawn = width * jax.random.normal(own_key, dims, jnp.float32)
    if split:
        drawn = drawn * block_levels(own_key, dims, split, -0.22, 0.18)
    return jnp.clip(drawn, -bound, bound).astype(kind)


def setup_inputs(seed: int = 0) -> dict:
    seeds = jax.random.split(jax.random.key(seed), 12)
    return {
        "patches": gaussian(seeds[0], (GH, GW, D), 1.0, 6.0, ((0, 16), (1, 8))),
        "norm_gain": jnp.clip(1.0 + 0.18 * jax.random.normal(seeds[1], (D,), jnp.float32), 0.1, 1.9),
        "query_weight": draw_query_weight(jax.random.fold_in(seeds[11], 71), 0),
        "key_weight": gaussian(seeds[3], (D, D), D ** -0.5, 0.15625, ((1, 8),)),
        "value_weight": gaussian(seeds[4], (D, D), D ** -0.5, 0.15625, ((1, 8),)),
        "out_weight": gaussian(seeds[5], (D, D), D ** -0.5, 0.15625),
        "merge_gain": jnp.clip(1.0 + 0.18 * jax.random.normal(seeds[6], (D,), jnp.float32), 0.1, 1.9),
        "up_weight": gaussian(seeds[7], (4 * D, HID), (4 * D) ** -0.5, 0.078125, ((1, 8),)),
        "up_bias": gaussian(seeds[8], (HID,), 0.5, 3.0, ((0, 8),), jnp.float32),
        "down_weight": gaussian(seeds[9], (HID, OUT), HID ** -0.5, 0.078125, ((0, 8),)),
        "down_bias": gaussian(seeds[10], (OUT,), 0.5, 3.0, (), jnp.float32),
    }


EPSILON = 1e-06

def rounded(tensor):
    return lax.optimization_barrier(tensor.astype(jnp.bfloat16)).astype(jnp.float32)

def layer_norm(tensor, gain_values):
    center = tensor - lax.optimization_barrier(jnp.mean(tensor, axis=-1, keepdims=True))
    spread = lax.optimization_barrier(jnp.mean(center * center, axis=-1, keepdims=True))
    return center * lax.rsqrt(spread + EPSILON) * gain_values.astype(jnp.float32)

def rotary(tensor, row_coord, col_coord):
    quarter = tensor.shape[-1] // 4
    half_dim = tensor.shape[-1] // 2
    frequency = 1.0 / 10000.0 ** (jnp.arange(quarter, dtype=jnp.float32) * 2.0 / half_dim)
    angles = jnp.concatenate([row_coord[:, None] * frequency, col_coord[:, None] * frequency], axis=-1)
    angles = jnp.concatenate([angles, angles], axis=-1)[:, None, :]
    rotated = jnp.concatenate([-tensor[..., half_dim:], tensor[..., :half_dim]], axis=-1)
    return tensor * jnp.cos(angles) + rotated * jnp.sin(angles)

def reference(patches, norm_gain, query_weight, key_weight, value_weight, out_weight, merge_gain, up_weight, up_bias, down_weight, down_bias):
    total_tokens = GH * GW
    tokens = patches.reshape(total_tokens, D).astype(jnp.float32)
    normed = rounded(layer_norm(tokens, norm_gain))
    places = jnp.arange(total_tokens, dtype=jnp.int32)
    row_coord = (places // GW).astype(jnp.float32)
    col_coord = (places % GW).astype(jnp.float32)
    queries = rounded(rotary(jnp.dot(normed, query_weight.astype(jnp.float32)).reshape(total_tokens, HEADS, HEAD_DIM), row_coord, col_coord))
    keys_all = rounded(rotary(jnp.dot(normed, key_weight.astype(jnp.float32)).reshape(total_tokens, HEADS, HEAD_DIM), row_coord, col_coord))
    values_all = rounded(jnp.dot(normed, value_weight.astype(jnp.float32))).reshape(total_tokens, HEADS, HEAD_DIM)
    score_scale = 1.0 / math.sqrt(HEAD_DIM)
    query_block_rows = math.gcd(total_tokens, 1024)

    def one_head(items):
        head_queries, head_keys, head_values = items

        def one_block(block_queries):
            scores = jnp.dot(block_queries, head_keys.T) * score_scale
            running_top = lax.optimization_barrier(jnp.max(scores, axis=-1, keepdims=True))
            weights = jnp.exp(scores - running_top)
            totals = lax.optimization_barrier(jnp.sum(weights, axis=-1, keepdims=True))
            return rounded(jnp.dot(rounded(weights), head_values) / totals)
        blocks = head_queries.reshape(total_tokens // query_block_rows, query_block_rows, HEAD_DIM)
        return lax.map(one_block, blocks).reshape(total_tokens, HEAD_DIM)
    attended = lax.map(one_head, (queries.transpose(1, 0, 2), keys_all.transpose(1, 0, 2), values_all.transpose(1, 0, 2)))
    attended = attended.transpose(1, 0, 2).reshape(total_tokens, D)
    group_size = D // N_COL
    mixed = jnp.zeros((total_tokens, D), jnp.float32)
    for group_index in range(N_COL):
        lower = group_index * group_size
        mixed = mixed + rounded(jnp.dot(attended[:, lower:lower + group_size], out_weight[lower:lower + group_size].astype(jnp.float32)))
    residual = tokens + mixed
    merge_in = rounded(layer_norm(residual, merge_gain))
    merged = merge_in.reshape(GH // 2, 2, GW // 2, 2, D).transpose(0, 2, 1, 3, 4).reshape(MTOK, 4 * D)
    hidden = rounded(jax.nn.gelu(jnp.dot(merged, up_weight.astype(jnp.float32)) + up_bias.astype(jnp.float32), approximate=False))
    hidden_group = HID // N_COL
    output_sum = jnp.zeros((MTOK, OUT), jnp.float32)
    for group_index in range(N_COL):
        lower = group_index * hidden_group
        output_sum = output_sum + rounded(jnp.dot(hidden[:, lower:lower + hidden_group], down_weight[lower:lower + hidden_group].astype(jnp.float32)))
    return (output_sum + down_bias.astype(jnp.float32)).astype(jnp.bfloat16)
```

```python
import functools
import math

import jax
import jax.numpy as jnp
import numpy as np
from jax import lax
from jax.experimental import pallas as pl
from jax.experimental.pallas import tpu as pltpu
from jax.sharding import Mesh
from jax.sharding import PartitionSpec as P

HEAD_DIM = 80
EPSILON = 1e-06
AXES = ("y", "zl", "c", "x", "zh")
SIZES = (4, 2, 2, 4, 2)
BF = jnp.bfloat16
F32 = jnp.float32
KEY_BLOCK = 2048
QUERY_BLOCK = 512
LIMIT = 2.0**64


def pairs(move):
    result = []
    for place in np.ndindex(*SIZES):
        there = dict(zip(AXES, place))
        there.update(move(there))
        target = tuple(there[a] % n for a, n in zip(AXES, SIZES))
        result.append(
            (int(np.ravel_multi_index(place, SIZES)), int(np.ravel_multi_index(target, SIZES)))
        )
    return result


def shift(axis, step):
    return pairs(lambda d: {axis: d[axis] + step})


def send(value, perm):
    return lax.ppermute(value, AXES, perm)


def vmem():
    return pl.BlockSpec(memory_space=pltpu.VMEM)


def smem():
    return pl.BlockSpec(memory_space=pltpu.SMEM)


def call(kernel, name, outs, ins, scratch=(), flops=0, nbytes=0, exps=0):
    specs = [smem() if k == "s" else vmem() for k, _ in ins]
    return pl.pallas_call(
        kernel,
        name=name,
        out_shape=outs,
        in_specs=specs,
        out_specs=jax.tree.map(lambda _: vmem(), outs),
        scratch_shapes=list(scratch),
        cost_estimate=pl.CostEstimate(flops=flops, bytes_accessed=nbytes, transcendentals=exps),
        compiler_params=pltpu.CompilerParams(vmem_limit_bytes=58 * 2**20),
    )(*[a for _, a in ins])


def norm(values, gain):
    center = values - jnp.mean(values, axis=-1, keepdims=True)
    spread = jnp.mean(center * center, axis=-1, keepdims=True)
    return center * lax.rsqrt(spread + EPSILON) * gain


def enter_kernel(patch_ref, gain_ref, token_ref, normed_ref):
    n = patch_ref.shape[0]
    r = lax.broadcasted_iota(jnp.int32, (n, n), 0)
    s = lax.broadcasted_iota(jnp.int32, (n, n), 1)
    a, b, u, w = r >> 6, (r >> 5) & 1, (r >> 3) & 3, r & 7
    source = (2 * u + a) * 16 + 2 * w + b
    pick = (source == s).astype(BF)
    tokens = jnp.dot(pick, patch_ref[...], preferred_element_type=F32)
    token_ref[...] = tokens.astype(BF)
    normed_ref[...] = norm(tokens, gain_ref[...]).astype(BF)


def project_kernel(c_ref, *refs):
    tiles, (wq, wk, wv, cos_ref, sin_ref, q_out, kv_out, other_out) = refs[:12], refs[12:]
    mine = pl.multiple_of(c_ref[0] * HEAD_DIM, 16)
    others = pl.multiple_of((1 - c_ref[0]) * HEAD_DIM, 16)
    weight = jnp.concatenate(
        [w[pl.ds(o, HEAD_DIM), :] for o in (mine, others) for w in (wq, wk, wv)], axis=0
    )
    half = HEAD_DIM // 2
    scale = math.log2(math.e) / math.sqrt(HEAD_DIM)
    groups = [tiles[0:2], tiles[2:4], tiles[4:8], tiles[8:12]]
    for g, group in enumerate(groups):
        rows = jnp.concatenate([t[...] for t in group], axis=0)
        mapped = lax.dot_general(
            weight, rows, (((1,), (1,)), ((), ())), preferred_element_type=F32
        )
        at = slice(g * 256, (g + 1) * 256)
        cos, sin = cos_ref[:, at], sin_ref[:, at]

        def turn(u):
            first, second = u[:half], u[half:]
            return jnp.concatenate([first * cos - second * sin, second * cos + first * sin], axis=0)

        part = [mapped[k * HEAD_DIM : (k + 1) * HEAD_DIM] for k in range(6)]
        q_out[:, at] = (turn(part[0]) * scale).astype(BF)
        kv_out[:HEAD_DIM, at] = turn(part[1]).astype(BF)
        kv_out[HEAD_DIM:, at] = part[2].astype(BF)
        other_out[:HEAD_DIM, at] = (turn(part[3]) * scale).astype(BF)
        other_out[HEAD_DIM : 2 * HEAD_DIM, at] = turn(part[4]).astype(BF)
        other_out[2 * HEAD_DIM :, at] = part[5].astype(BF)


def split_rows(m):
    hi = m.astype(BF)
    rest = m - hi.astype(F32)
    mid = rest.astype(BF)
    low = (rest - mid.astype(F32)).astype(BF)
    pad = jnp.zeros((13, m.shape[1]), BF)
    return jnp.concatenate([-hi, -mid, -low, pad], axis=0)


def attend_chunks(chunks, q_ref, m_ref, base_ref, o_ref, k_all, v_all, flag):
    keys = k_all.shape[0]
    queries = q_ref.shape[1]
    step = min(KEY_BLOCK, keys)
    at = 0
    for ref in chunks:
        n = ref.shape[1]
        ones = jnp.ones((16, n), BF)
        k_all[at : at + n, :] = jnp.concatenate([ref[:HEAD_DIM, :], ones], axis=0).T
        v_all[:, at : at + n] = jnp.concatenate([ref[HEAD_DIM:, :], ones], axis=0)
        at += n
    flag[0] = 1

    def attempt(tries, carry):
        @pl.when(flag[0] == 1)
        def _():
            o_ref[...] = jnp.zeros_like(o_ref) if base_ref is None else base_ref[...]

            def block(j, carry):
                rows = pl.ds(pl.multiple_of(j * step, step), step)
                for i in range(queries // QUERY_BLOCK):
                    cols = slice(i * QUERY_BLOCK, (i + 1) * QUERY_BLOCK)
                    s = jnp.dot(k_all[rows, :], q_ref[:, cols], preferred_element_type=F32)
                    p = jnp.exp2(s).astype(BF)
                    o_ref[:, cols] += jnp.dot(v_all[:, rows], p, preferred_element_type=F32)
                return carry

            lax.fori_loop(0, keys // step, block, 0)
            mass = o_ref[HEAD_DIM : HEAD_DIM + 8, :]
            bad = jnp.max(jnp.where(mass < LIMIT, 0.0, 1.0)) > 0.0
            flag[0] = jnp.where(jnp.logical_and(bad, tries == 0), 1, 0)

            @pl.when(flag[0] == 1)
            def _():
                def top_block(j, carry):
                    rows = pl.ds(pl.multiple_of(j * 512, 512), 512)
                    for i in range(queries // QUERY_BLOCK):
                        cols = slice(i * QUERY_BLOCK, (i + 1) * QUERY_BLOCK)
                        s = jnp.dot(k_all[rows, :], q_ref[:, cols], preferred_element_type=F32)
                        m_ref[1:2, cols] = jnp.maximum(
                            m_ref[1:2, cols], jnp.max(s, axis=0, keepdims=True)
                        )
                    return carry

                m_ref[1:2, :] = jnp.zeros((1, queries), F32)
                lax.fori_loop(0, keys // 512, top_block, 0)
                rise = m_ref[1:2, :]
                fresh = m_ref[0:1, :] + rise
                m_ref[0:1, :] = fresh
                q_ref[HEAD_DIM:, :] = split_rows(fresh)
                if base_ref is not None:
                    base_ref[...] = base_ref[...] * jnp.exp2(-rise)

        return carry

    lax.fori_loop(0, 2, attempt, 0)


def first_kernel(own_q, other_q, kv_ref, q_ref, m_ref, o_ref, k_all, v_all, flag):
    n = own_q.shape[1]
    q_ref[:HEAD_DIM, :n] = own_q[...]
    q_ref[:HEAD_DIM, n:] = other_q[:HEAD_DIM, :]
    some = kv_ref[:HEAD_DIM, :512].T
    for i in range(2 * n // QUERY_BLOCK):
        cols = slice(i * QUERY_BLOCK, (i + 1) * QUERY_BLOCK)
        s = jnp.dot(some, q_ref[:HEAD_DIM, cols], preferred_element_type=F32)
        m_ref[:, cols] = jnp.broadcast_to(jnp.max(s, axis=0, keepdims=True), (8, QUERY_BLOCK))
    q_ref[HEAD_DIM:, :] = split_rows(m_ref[0:1, :])
    attend_chunks([kv_ref], q_ref, m_ref, None, o_ref, k_all, v_all, flag)


def next_kernel(count, *refs):
    chunks, rest = refs[:count], refs[count:]
    q_in, m_in, base_in, q_ref, m_ref, o_ref, base, k_all, v_all, flag = rest
    q_ref[...] = q_in[...]
    m_ref[...] = m_in[...]
    base[...] = base_in[...]
    attend_chunks(chunks, q_ref, m_ref, base, o_ref, k_all, v_all, flag)


def last_kernel(count, place, *refs):
    chunks, rest = refs[:count], refs[count:]
    q_in, m_in, base_in, out_ref, q_ref, m_ref, o_ref, base, k_all, v_all, flag = rest
    q_ref[...] = q_in[...]
    m_ref[...] = m_in[...]
    base[...] = base_in[...]
    attend_chunks(chunks, q_ref, m_ref, base, o_ref, k_all, v_all, flag)
    for s in range(out_ref.shape[0]):
        cols = slice(s * 128, (s + 1) * 128)
        mass = o_ref[HEAD_DIM : HEAD_DIM + 1, cols]
        out_ref[place[s]] = (o_ref[:HEAD_DIM, cols] / mass).astype(BF)


def mix_kernel(att_ref, weight_ref, token_ref, gain_ref, out_ref):
    att = att_ref[...].reshape(-1, att_ref.shape[-1])
    mixed = lax.dot_general(
        att, weight_ref[...], (((0,), (0,)), ((), ())), preferred_element_type=F32
    )
    out_ref[...] = norm(token_ref[...].astype(F32) + mixed, gain_ref[...]).astype(BF)


def up_kernel(place_ref, *refs):
    tiles, (weight_ref, bias_ref, out_ref) = refs[:12], refs[12:]
    width = weight_ref.shape[0] // 4
    total = None
    for q in range(4):
        rows = [t[q * 32 : (q + 1) * 32, :] for t in tiles[:4]]
        for k in range(4, 12, 2):
            rows.append(tiles[k + q // 2][(q % 2) * 32 : (q % 2 + 1) * 32, :])
        lhs = jnp.concatenate(rows, axis=0)
        part = jnp.dot(
            lhs, weight_ref[q * width : (q + 1) * width, :], preferred_element_type=F32
        )
        total = part if total is None else total + part
    z = total + bias_ref[...]
    hidden = (0.5 * z * (1.0 + lax.erf(z * (1.0 / math.sqrt(2.0))))).astype(BF)
    n = hidden.shape[0]
    pick = (lax.broadcasted_iota(jnp.int32, (n, n), 0) == place_ref[...]).astype(BF)
    out_ref[...] = jnp.dot(pick, hidden, preferred_element_type=F32).astype(BF)


def spread(own, axis, across, dim, size):
    forward, backward = shift(axis, 1), shift(axis, -1)
    half = size // 2
    low = lambda t: lax.slice_in_dim(t, 0, half, axis=dim)
    high = lambda t: lax.slice_in_dim(t, half, size, axis=dim)
    join = lambda *t: lax.concatenate(t, dim)
    plus = send(own, forward)
    minus = send(own, backward)
    mirror = send(own, across)
    first = (plus, minus, mirror)
    ahead = send(join(low(plus), low(mirror)), forward)
    behind = send(join(high(minus), low(mirror)), backward)
    side = send(join(high(plus), high(minus)), across)
    two_low, mirror_plus_low = low(ahead), high(ahead)
    two_high, mirror_minus_low = low(behind), high(behind)
    mirror_plus_high, mirror_minus_high = low(side), high(side)
    second = (
        (two_low, two_high),
        (mirror_plus_low, mirror_plus_high),
        (mirror_minus_low, mirror_minus_high),
    )
    far_low = send(mirror_plus_low, forward)
    far_high = send(mirror_minus_high, backward)
    return first, second, (far_low, far_high)


def shards(
    patches,
    norm_gain,
    query_weight,
    key_weight,
    value_weight,
    out_weight,
    merge_gain,
    up_weight,
    up_bias,
    down_weight,
    down_bias,
):
    band_height, tile_width, model_width = patches.shape
    tile = band_height * tile_width
    band = tile * 8
    y, zl, c = lax.axis_index("y"), lax.axis_index("zl"), lax.axis_index("c")
    x, zh = lax.axis_index("x"), lax.axis_index("zh")
    row_index = (y * 2 + zl) * 2 + c
    sds = jax.ShapeDtypeStruct

    slot_x = jnp.stack([x, x - 1, x + 1, x, x + 2, x - 1, x + 1, x + 2]) % 4
    slot_z = jnp.stack([zh, zh, zh, 1 - zh, zh, 1 - zh, 1 - zh, 1 - zh])
    slot_col = (slot_x * 2 + slot_z).astype(jnp.int32)
    local = np.arange(tile)
    local_i = 2 * ((local >> 3) & 3) + (local >> 6)
    local_j = 2 * (local & 7) + ((local >> 5) & 1)
    row_coord = (row_index * band_height + jnp.tile(local_i, 8)).astype(F32)
    col_coord = (slot_col[:, None] * tile_width + local_j[None, :]).astype(F32).reshape(-1)
    frequency = 1.0 / 10000.0 ** (
        jnp.arange(HEAD_DIM // 4, dtype=F32) * 2.0 / (HEAD_DIM // 2)
    )
    angles = jnp.concatenate(
        [frequency[:, None] * row_coord[None, :], frequency[:, None] * col_coord[None, :]], axis=0
    )
    cos, sin = jnp.cos(angles), jnp.sin(angles)

    tokens, normed = call(
        enter_kernel,
        "enter",
        (sds((tile, model_width), BF), sds((tile, model_width), BF)),
        [("v", patches.reshape(tile, model_width)), ("v", norm_gain.reshape(1, -1))],
    )
    mirror_x = pairs(lambda d: {"zh": 1 - d["zh"]})
    first, second, far = spread(normed, "x", mirror_x, 0, tile)
    flat = [normed, *first, *[p for pair in second for p in pair], *far]
    q_own, kv_own, other = call(
        project_kernel,
        "project",
        (sds((HEAD_DIM, band), BF), sds((2 * HEAD_DIM, band), BF), sds((3 * HEAD_DIM, band), BF)),
        [("s", c.reshape(1).astype(jnp.int32))]
        + [("v", t) for t in flat]
        + [("v", query_weight.T), ("v", key_weight.T), ("v", value_weight.T), ("v", cos), ("v", sin)],
        flops=2 * band * model_width * 480,
    )
    swapped = send(other, pairs(lambda d: {"c": 1 - d["c"]}))
    kv = jnp.concatenate([kv_own, swapped[HEAD_DIM:]], axis=1)
    mirror_y = pairs(lambda d: {"zl": 1 - d["zl"]})
    near, middle, distant = spread(kv, "y", mirror_y, 1, 2 * band)
    n = 2 * band
    q_shape, m_shape, o_shape = sds((96, n), BF), sds((8, n), F32), sds((96, n), F32)

    def scratch(keys):
        return [pltpu.VMEM((keys, 96), BF), pltpu.VMEM((96, keys), BF), pltpu.SMEM((1,), jnp.int32)]

    work = lambda keys: dict(flops=2 * n * keys * 512, exps=n * keys, nbytes=4 * n * 96)
    q, m, o = call(
        first_kernel,
        "attend0",
        (q_shape, m_shape, o_shape),
        [("v", q_own), ("v", swapped), ("v", kv)],
        scratch(n),
        **work(n),
    )
    state = (q, m, o)
    base = pltpu.VMEM((96, n), F32)
    middle_flat = [p for pair in middle for p in pair]
    for name, chunks in (("attend1", list(near)), ("attend2", middle_flat)):
        keys = sum(t.shape[1] for t in chunks)
        state = call(
            functools.partial(next_kernel, len(chunks)),
            name,
            (q_shape, m_shape, o_shape),
            [("v", t) for t in chunks] + [("v", t) for t in state],
            [base] + scratch(keys),
            **work(keys),
        )
    place = jnp.concatenate([slot_col * 2 + c, slot_col * 2 + 1 - c]).astype(jnp.int32)
    attended = call(
        functools.partial(last_kernel, 2),
        "attend3",
        sds((16, HEAD_DIM, tile), BF),
        [("s", place)] + [("v", t) for t in distant] + [("v", t) for t in state],
        [pltpu.VMEM((96, n), BF), pltpu.VMEM((8, n), F32), pltpu.VMEM((96, n), F32), base]
        + scratch(n),
        **work(n),
    )
    gathered = lax.all_to_all(attended, ("x", "zh", "c"), 0, 0, tiled=True)
    merge_in = call(
        mix_kernel,
        "mix",
        sds((tile, model_width), BF),
        [
            ("v", gathered),
            ("v", out_weight),
            ("v", tokens),
            ("v", merge_gain.reshape(1, -1)),
        ],
    )
    first, second, far = spread(merge_in, "x", mirror_x, 0, tile)
    flat = [merge_in, *first, *[p for pair in second for p in pair], *far]
    raster = np.arange(32)
    target = (
        (raster >> 3)[None, :] * 64 + slot_col[:, None] * 8 + (raster & 7)[None, :]
    ).astype(jnp.int32).reshape(1, -1)
    hidden = call(
        up_kernel,
        "up",
        sds((256, up_weight.shape[1]), BF),
        [("v", target)]
        + [("v", t) for t in flat]
        + [("v", up_weight), ("v", up_bias.reshape(1, -1))],
        flops=2 * 256 * 5120 * 640,
    )
    return scatter_output(hidden, down_weight, down_bias, x, zh, mirror_x)


def scatter_output(hidden, down_weight, down_bias, x, zh, mirror):
    parts = 2
    width = down_weight.shape[1]
    forward, backward = shift("x", 1), shift("x", -1)
    pieces = []
    for k in range(parts):
        size = width // parts
        cols = slice(k * size, (k + 1) * size)
        part = jnp.dot(hidden, down_weight[:, cols], preferred_element_type=F32).astype(BF)
        part = part.reshape(4, 64, size)
        pick = lambda d: lax.dynamic_index_in_dim(part, (x + d) % 4, 0, keepdims=False)
        half = size // 2
        far = pick(2)
        from_behind = send(far[:, :half], forward)
        from_ahead = send(far[:, half:], backward)
        after, before = pick(1), pick(3)
        onward = jnp.concatenate(
            [
                (after[:, :half].astype(F32) + from_behind.astype(F32)).astype(BF),
                after[:, half:],
            ],
            axis=1,
        )
        back = jnp.concatenate(
            [
                before[:, :half],
                (before[:, half:].astype(F32) + from_ahead.astype(F32)).astype(BF),
            ],
            axis=1,
        )
        got_behind = send(onward, forward)
        got_ahead = send(back, backward)
        total = pick(0).astype(F32) + got_behind.astype(F32) + got_ahead.astype(F32)
        total = total.reshape(2, 32, size)
        give = lax.dynamic_index_in_dim(total, 1 - zh, 0, keepdims=False).astype(BF)
        keep = lax.dynamic_index_in_dim(total, zh, 0, keepdims=False)
        got = send(give, mirror)
        pieces.append((keep + got.astype(F32) + down_bias[None, cols]).astype(BF))
    return jnp.concatenate(pieces, axis=1)


def solution(mesh):
    fine = Mesh(mesh.devices.reshape(SIZES), AXES)
    row, col = ("y", "zl", "c"), ("x", "zh")
    placed = (
        P(row, col, None),
        P(),
        P(None, col),
        P(None, col),
        P(None, col),
        P(),
        P(),
        P(None, col),
        P(col),
        P(col, None),
        P(),
    )
    return jax.shard_map(
        shards, mesh=fine, in_specs=placed, out_specs=P(row + col, None), check_vma=False
    )
```

```python
import functools
import math

import jax
import jax.numpy as jnp
import numpy as np
from jax import lax
from jax.experimental import pallas as pl
from jax.experimental.pallas import tpu as pltpu
from jax.sharding import Mesh
from jax.sharding import PartitionSpec as P

HEAD_DIM = 80
EPSILON = 1e-06
AXES = ("y", "zl", "c", "x", "zh")
SIZES = (4, 2, 2, 4, 2)
BF = jnp.bfloat16
F32 = jnp.float32
QUERY_BLOCK = 512
LIMIT = 2.0**64


def pairs(move):
    result = []
    for place in np.ndindex(*SIZES):
        there = dict(zip(AXES, place))
        there.update(move(there))
        target = tuple(there[a] % n for a, n in zip(AXES, SIZES))
        result.append(
            (int(np.ravel_multi_index(place, SIZES)), int(np.ravel_multi_index(target, SIZES)))
        )
    return result


def shift(axis, step):
    return pairs(lambda d: {axis: d[axis] + step})


def send(value, perm):
    return lax.ppermute(value, AXES, perm)


def vmem():
    return pl.BlockSpec(memory_space=pltpu.VMEM)


def smem():
    return pl.BlockSpec(memory_space=pltpu.SMEM)


def call(kernel, name, outs, ins, scratch=(), flops=0, nbytes=0, exps=0):
    specs = [smem() if k == "s" else vmem() for k, _ in ins]
    return pl.pallas_call(
        kernel,
        name=name,
        out_shape=outs,
        in_specs=specs,
        out_specs=jax.tree.map(lambda _: vmem(), outs),
        scratch_shapes=list(scratch),
        cost_estimate=pl.CostEstimate(flops=flops, bytes_accessed=nbytes, transcendentals=exps),
        compiler_params=pltpu.CompilerParams(vmem_limit_bytes=58 * 2**20),
    )(*[a for _, a in ins])


def norm(values, gain):
    center = values - jnp.mean(values, axis=-1, keepdims=True)
    spread = jnp.mean(center * center, axis=-1, keepdims=True)
    return center * lax.rsqrt(spread + EPSILON) * gain


def project_kernel(c_ref, *refs):
    tiles, rest = refs[:12], refs[12:]
    gain_ref, wq, wk, wv, cos_ref, sin_ref, q_out, kv_out, other_out = rest
    mine = pl.multiple_of(c_ref[0] * HEAD_DIM, 16)
    others = pl.multiple_of((1 - c_ref[0]) * HEAD_DIM, 16)
    weight = jnp.concatenate(
        [w[pl.ds(o, HEAD_DIM), :] for o in (mine, others) for w in (wq, wk, wv)], axis=0
    )
    half = HEAD_DIM // 2
    scale = math.log2(math.e) / math.sqrt(HEAD_DIM)
    groups = [tiles[0:2], tiles[2:4], tiles[4:8], tiles[8:12]]
    for g, group in enumerate(groups):
        rows = jnp.concatenate([t[...] for t in group], axis=0).astype(F32)
        rows = norm(rows, gain_ref[...]).astype(BF)
        mapped = lax.dot_general(
            weight, rows, (((1,), (1,)), ((), ())), preferred_element_type=F32
        )
        at = slice(g * 256, (g + 1) * 256)
        cos, sin = cos_ref[:, at], sin_ref[:, at]

        def turn(u):
            first, second = u[:half], u[half:]
            return jnp.concatenate([first * cos - second * sin, second * cos + first * sin], axis=0)

        part = [mapped[k * HEAD_DIM : (k + 1) * HEAD_DIM] for k in range(6)]
        q_out[:, at] = (turn(part[0]) * scale).astype(BF)
        kv_out[:HEAD_DIM, at] = turn(part[1]).astype(BF)
        kv_out[HEAD_DIM:, at] = part[2].astype(BF)
        other_out[:HEAD_DIM, at] = (turn(part[3]) * scale).astype(BF)
        other_out[HEAD_DIM : 2 * HEAD_DIM, at] = turn(part[4]).astype(BF)
        other_out[2 * HEAD_DIM :, at] = part[5].astype(BF)


def split_rows(m):
    hi = m.astype(BF)
    rest = m - hi.astype(F32)
    mid = rest.astype(BF)
    low = (rest - mid.astype(F32)).astype(BF)
    pad = jnp.zeros((13, m.shape[1]), BF)
    return jnp.concatenate([-hi, -mid, -low, pad], axis=0)


def attend_chunks(chunks, q_ref, m_ref, o_ref, k_all, v_all, flag):
    keys = k_all.shape[0]
    queries = q_ref.shape[1]
    step = keys if keys <= 2048 else max(d for d in (2048, 1536, 1024) if keys % d == 0)
    turns = queries // (2 * QUERY_BLOCK)
    at = 0
    for ref in chunks:
        n = ref.shape[1]
        ones = jnp.ones((16, n), BF)
        k_all[at : at + n, :] = jnp.concatenate([ref[-2 * HEAD_DIM : -HEAD_DIM, :], ones], axis=0).T
        v_all[:, at : at + n] = jnp.concatenate([ref[-HEAD_DIM:, :], ones], axis=0)
        at += n
    flag[0] = 1

    def attempt(tries, carry):
        @pl.when(flag[0] == 1)
        def _():
            o_ref[...] = jnp.zeros_like(o_ref)

            def block(t, carry):
                rows = pl.ds(pl.multiple_of((t // turns) * step, step), step)
                for i in range(2):
                    col = (t % turns) * (2 * QUERY_BLOCK) + i * QUERY_BLOCK
                    cols = pl.ds(pl.multiple_of(col, QUERY_BLOCK), QUERY_BLOCK)
                    s = jnp.dot(k_all[rows, :], q_ref[:, cols], preferred_element_type=F32)
                    p = jnp.exp2(s).astype(BF)
                    o_ref[:, cols] += jnp.dot(v_all[:, rows], p, preferred_element_type=F32)
                return carry

            lax.fori_loop(0, keys // step * turns, block, 0)
            mass = o_ref[HEAD_DIM : HEAD_DIM + 8, :]
            bad = jnp.max(jnp.where(mass < LIMIT, 0.0, 1.0)) > 0.0
            flag[0] = jnp.where(jnp.logical_and(bad, tries == 0), 1, 0)

            @pl.when(flag[0] == 1)
            def _():
                m_ref[1:2, :] = jnp.zeros((1, queries), F32)

                def top_block(t, carry):
                    rows = pl.ds(pl.multiple_of((t // 8) * 512, 512), 512)
                    cols = pl.ds(pl.multiple_of((t % 8) * 256, 256), 256)
                    s = jnp.dot(k_all[rows, :], q_ref[:, cols], preferred_element_type=F32)
                    m_ref[1:2, cols] = jnp.maximum(
                        m_ref[1:2, cols], jnp.max(s, axis=0, keepdims=True)
                    )
                    return carry

                lax.fori_loop(0, keys // 512 * (queries // 256), top_block, 0)
                fresh = m_ref[0:1, :] + m_ref[1:2, :]
                m_ref[0:1, :] = fresh
                q_ref[HEAD_DIM:, :] = split_rows(fresh)

        return carry

    lax.fori_loop(0, 2, attempt, 0)


def first_kernel(own_q, swapped, kv_ref, q_out, start_out, m_ref, o_ref, q_ref, k_all, v_all, flag):
    n = own_q.shape[1]
    q_ref[:HEAD_DIM, :n] = own_q[...]
    q_ref[:HEAD_DIM, n:] = swapped[:HEAD_DIM, :]
    some = kv_ref[:HEAD_DIM, :512].T

    def start(i, carry):
        cols = pl.ds(pl.multiple_of(i * QUERY_BLOCK, QUERY_BLOCK), QUERY_BLOCK)
        s = jnp.dot(some, q_ref[:HEAD_DIM, cols], preferred_element_type=F32)
        m_ref[:, cols] = jnp.broadcast_to(jnp.max(s, axis=0, keepdims=True), (8, QUERY_BLOCK))
        return carry

    lax.fori_loop(0, 2 * n // QUERY_BLOCK, start, 0)
    q_ref[HEAD_DIM:, :] = split_rows(m_ref[0:1, :])
    q_out[...] = q_ref[...]
    start_out[...] = m_ref[...]
    attend_chunks([kv_ref], q_ref, m_ref, o_ref, k_all, v_all, flag)


def next_kernel(count, *refs):
    chunks, rest = refs[:count], refs[count:]
    q_in, m_in, m_ref, o_ref, q_ref, k_all, v_all, flag = rest
    q_ref[...] = q_in[...]
    m_ref[...] = m_in[...]
    attend_chunks(chunks, q_ref, m_ref, o_ref, k_all, v_all, flag)


def last_kernel(count, done, place, *refs):
    chunks, rest = refs[:count], refs[count:]
    q_in, m_in = rest[:2]
    tops, sums = rest[2 : 2 + done], rest[2 + done : 2 + 2 * done]
    own_ref, swap_ref, q_ref, m_ref, o_ref, k_all, v_all, flag = rest[2 + 2 * done :]
    q_ref[...] = q_in[...]
    m_ref[...] = m_in[...]
    attend_chunks(chunks, q_ref, m_ref, o_ref, k_all, v_all, flag)
    top = m_ref[0:1, :]
    for t in tops:
        top = jnp.maximum(top, t[0:1, :])
    total = o_ref[...] * jnp.exp2(m_ref[0:1, :] - top)
    for t, o in zip(tops, sums):
        total = total + o[...] * jnp.exp2(t[0:1, :] - top)
    half = total.shape[1] // 2
    for out_ref, lower in ((own_ref, 0), (swap_ref, half)):
        for s in range(half // 128):
            cols = slice(lower + s * 128, lower + (s + 1) * 128)
            mass = total[HEAD_DIM : HEAD_DIM + 1, cols]
            target = pl.ds(pl.multiple_of(place[s] * 128, 128), 128)
            out_ref[:, target] = (total[:HEAD_DIM, cols] / mass).astype(BF)


def merge_kernel(col_ref, c_ref, *refs):
    pieces, tiles, rest = refs[:12], refs[12:24], refs[24:]
    out_weight, gain_ref, up_weight, bias_ref, place_a, place_b = rest[:6]
    hidden_a, hidden_b, att_all, token_all, mixed_all, merged = rest[6:]
    starts = [0, 0, 0, 0, 0, 80, 0, 80, 0, 80, 0, 80]
    slots = [0, 1, 2, 3, 4, 4, 5, 5, 6, 6, 7, 7]
    c = c_ref[0]
    for piece, tile, slot, lower in zip(pieces, tiles, slots, starts):
        first = 80 if lower else 0
        for part in range(piece.shape[0] // 80):
            odd = (lower + part * 80) // 80
            spot = col_ref[slot] * 160 + (c if odd == 0 else 1 - c) * 80
            att_all[pl.ds(pl.multiple_of(spot, 16), 80), :] = piece[part * 80 : (part + 1) * 80, :]
        row = slot * 128 + (64 if lower else 0)
        token_all[row : row + tile.shape[0], :] = tile[...]
    width = out_weight.shape[1]

    def project(i, carry):
        spot = pl.ds(pl.multiple_of(i * 256, 256), 256)
        lhs = att_all[:, spot].T
        mixed_all[spot, :] = jnp.dot(lhs, out_weight[...], preferred_element_type=F32)
        return carry

    lax.fori_loop(0, 4, project, 0)
    r = lax.broadcasted_iota(jnp.int32, (128, 128), 0)
    t = lax.broadcasted_iota(jnp.int32, (128, 128), 1)
    a, b, u, w = r >> 6, (r >> 5) & 1, (r >> 3) & 3, r & 7
    pick = ((2 * u + a) * 16 + 2 * w + b == t).astype(BF)

    def settle(s, carry):
        spot = pl.ds(pl.multiple_of(col_ref[s] * 128, 128), 128)
        own = pl.ds(pl.multiple_of(s * 128, 128), 128)
        residual = token_all[own, :].astype(F32) + mixed_all[spot, :]
        normed = norm(residual, gain_ref[...]).astype(BF)
        ordered = jnp.dot(pick, normed, preferred_element_type=F32).astype(BF)
        for q in range(4):
            merged[q, pl.ds(pl.multiple_of(s * 32, 32), 32), :] = ordered[q * 32 : (q + 1) * 32]
        return carry

    lax.fori_loop(0, 8, settle, 0)
    z = bias_ref[...]
    for q in range(4):
        z = z + jnp.dot(
            merged[q], up_weight[q * width : (q + 1) * width, :], preferred_element_type=F32
        )
    hidden = (0.5 * z * (1.0 + lax.erf(z * (1.0 / math.sqrt(2.0))))).astype(BF)
    n = hidden.shape[0]
    rows = lax.broadcasted_iota(jnp.int32, (n, n), 0)
    for place, out in ((place_a, hidden_a), (place_b, hidden_b)):
        out[...] = jnp.dot(
            (rows == place[...]).astype(BF), hidden, preferred_element_type=F32
        ).astype(BF)


def spread(own, axis, across, dim, size):
    forward, backward = shift(axis, 1), shift(axis, -1)
    half = size // 2
    low = lambda t: lax.slice_in_dim(t, 0, half, axis=dim)
    high = lambda t: lax.slice_in_dim(t, half, size, axis=dim)
    join = lambda *t: lax.concatenate(t, dim)
    plus = send(own, forward)
    minus = send(own, backward)
    mirror = send(own, across)
    ahead = send(join(low(plus), low(mirror)), forward)
    behind = send(join(high(minus), low(mirror)), backward)
    side = send(join(high(plus), high(minus)), across)
    two_low, mirror_plus_low = low(ahead), high(ahead)
    two_high, mirror_minus_low = low(behind), high(behind)
    mirror_plus_high, mirror_minus_high = low(side), high(side)
    far_low = send(mirror_plus_low, forward)
    far_high = send(mirror_minus_high, backward)
    return (
        own,
        plus,
        minus,
        mirror,
        two_low,
        two_high,
        mirror_plus_low,
        mirror_plus_high,
        mirror_minus_low,
        mirror_minus_high,
        far_low,
        far_high,
    )


def shards(
    patches,
    norm_gain,
    query_weight,
    key_weight,
    value_weight,
    out_weight,
    merge_gain,
    up_weight,
    up_bias,
    down_weight,
    down_bias,
):
    band_height, tile_width, model_width = patches.shape
    tile = band_height * tile_width
    band = tile * 8
    y, zl, c = lax.axis_index("y"), lax.axis_index("zl"), lax.axis_index("c")
    x, zh = lax.axis_index("x"), lax.axis_index("zh")
    row_index = (y * 2 + zl) * 2 + c
    sds = jax.ShapeDtypeStruct

    slot_x = jnp.stack([x, x - 1, x + 1, x, x + 2, x - 1, x + 1, x + 2]) % 4
    slot_z = jnp.stack([zh, zh, zh, 1 - zh, zh, 1 - zh, 1 - zh, 1 - zh])
    slot_col = (slot_x * 2 + slot_z).astype(jnp.int32)
    local = np.arange(tile)
    row_coord = (row_index * band_height + jnp.tile(local // tile_width, 8)).astype(F32)
    col_coord = (
        (slot_col[:, None] * tile_width + (local % tile_width)[None, :]).astype(F32).reshape(-1)
    )
    frequency = 1.0 / 10000.0 ** (
        jnp.arange(HEAD_DIM // 4, dtype=F32) * 2.0 / (HEAD_DIM // 2)
    )
    angles = jnp.concatenate(
        [frequency[:, None] * row_coord[None, :], frequency[:, None] * col_coord[None, :]], axis=0
    )
    cos, sin = jnp.cos(angles), jnp.sin(angles)

    mirror_x = pairs(lambda d: {"zh": 1 - d["zh"]})
    tokens = patches.reshape(tile, model_width)
    tiles = spread(tokens, "x", mirror_x, 0, tile)
    q_own, kv_own, other = call(
        project_kernel,
        "project",
        (sds((HEAD_DIM, band), BF), sds((2 * HEAD_DIM, band), BF), sds((3 * HEAD_DIM, band), BF)),
        [("s", c.reshape(1).astype(jnp.int32))]
        + [("v", t) for t in tiles]
        + [("v", norm_gain.reshape(1, -1))]
        + [("v", query_weight.T), ("v", key_weight.T), ("v", value_weight.T), ("v", cos), ("v", sin)],
        flops=2 * band * model_width * 480,
    )
    n = 2 * band
    swap = pairs(lambda d: {"c": 1 - d["c"]})
    mirror_y = pairs(lambda d: {"zl": 1 - d["zl"]})
    swapped = send(other, swap)
    kv = jnp.concatenate([kv_own, swapped[HEAD_DIM:]], axis=1)
    chunks = spread(kv, "y", mirror_y, 1, n)
    groups = (chunks[1:4], chunks[4:10], chunks[10:])
    q_shape, m_shape, o_shape = sds((96, n), BF), sds((8, n), F32), sds((96, n), F32)

    def scratch(keys):
        return [
            pltpu.VMEM((96, n), BF),
            pltpu.VMEM((keys, 96), BF),
            pltpu.VMEM((96, keys), BF),
            pltpu.SMEM((1,), jnp.int32),
        ]

    work = lambda keys: dict(flops=2 * n * keys * 512, exps=n * keys, nbytes=4 * n * 96)
    q, start, top, part = call(
        first_kernel,
        "attend0",
        (q_shape, m_shape, m_shape, o_shape),
        [("v", q_own), ("v", swapped), ("v", kv)],
        scratch(n),
        **work(n),
    )
    tops, parts = [top], [part]
    for index, chunks in enumerate(groups[:-1]):
        keys = sum(t.shape[1] for t in chunks)
        top, part = call(
            functools.partial(next_kernel, len(chunks)),
            f"attend{index + 1}",
            (m_shape, o_shape),
            [("v", t) for t in chunks] + [("v", q), ("v", start)],
            scratch(keys),
            **work(keys),
        )
        tops.append(top)
        parts.append(part)
    final = scratch(n)
    half_shape = sds((HEAD_DIM, band), BF)
    attended, partner = call(
        functools.partial(last_kernel, 2, len(tops)),
        "attend3",
        (half_shape, half_shape),
        [("s", slot_col)] + [("v", t) for t in (*groups[-1], q, start, *tops, *parts)],
        [final[0], pltpu.VMEM((8, n), F32), pltpu.VMEM((96, n), F32), *final[1:]],
        **work(n),
    )
    attended = jnp.concatenate([attended, send(partner, swap)], axis=0)
    pieces = spread(attended, "x", mirror_x, 0, 2 * HEAD_DIM)
    spot = np.arange(32)
    raster = (spot >> 3)[None, :] * 64 + slot_col[:, None] * 8 + (spot & 7)[None, :]
    owner = raster >> 5
    ahead = ((owner >> 1) - x) & 3
    other_half = (owner & 1) ^ zh
    row_a = ahead * 64 + other_half * 32 + (raster & 31)
    row_b = other_half * 128 + ahead * 32 + (raster & 31)
    hidden_a, hidden_b = call(
        merge_kernel,
        "merge",
        (sds((256, up_weight.shape[1]), BF),) * 2,
        [("s", slot_col), ("s", c.reshape(1).astype(jnp.int32))]
        + [("v", t) for t in (*pieces, *tiles)]
        + [
            ("v", out_weight),
            ("v", merge_gain.reshape(1, -1)),
            ("v", up_weight),
            ("v", up_bias.reshape(1, -1)),
            ("v", row_a.astype(jnp.int32).reshape(1, -1)),
            ("v", row_b.astype(jnp.int32).reshape(1, -1)),
        ],
        [
            pltpu.VMEM((model_width, band), BF),
            pltpu.VMEM((band, model_width), BF),
            pltpu.VMEM((band, model_width), F32),
            pltpu.VMEM((4, 256, model_width), BF),
        ],
        flops=2 * 256 * 5120 * 640 + 2 * band * model_width * model_width,
    )
    return scatter_output(hidden_a, hidden_b, down_weight, down_bias, mirror_x)


def ring(block, rows):
    forward, backward = shift("x", 1), shift("x", -1)
    half = block.shape[1] // 2
    part = lambda k: block[k * rows : (k + 1) * rows]
    ahead, behind, far = part(1), part(3), part(2)
    from_behind = send(far[:, :half], forward)
    from_ahead = send(far[:, half:], backward)
    add = lambda p, q: (p.astype(F32) + q.astype(F32)).astype(BF)
    onward = jnp.concatenate([add(ahead[:, :half], from_behind), ahead[:, half:]], axis=1)
    back = jnp.concatenate([behind[:, :half], add(behind[:, half:], from_ahead)], axis=1)
    got_behind, got_ahead = send(onward, forward), send(back, backward)
    return part(0).astype(F32) + got_behind.astype(F32) + got_ahead.astype(F32)


def scatter_output(hidden_a, hidden_b, down_weight, down_bias, mirror):
    width = down_weight.shape[1]
    split = 4608
    with jax.named_scope("down_b"):
        part_b = jnp.dot(
            hidden_b, down_weight[:, split:], preferred_element_type=F32
        ).astype(BF)
    with jax.named_scope("mirror_b"):
        got_b = send(part_b[128:], mirror)
    with jax.named_scope("down_a"):
        part_a = jnp.dot(
            hidden_a, down_weight[:, :split], preferred_element_type=F32
        ).astype(BF)
    total_a = ring(part_a, 64)
    got_a = send(total_a[32:].astype(BF), mirror)
    block_b = (part_b[:128].astype(F32) + got_b.astype(F32)).astype(BF)
    total_b = ring(block_b, 32)
    total_a = total_a[:32] + got_a.astype(F32)
    return (jnp.concatenate([total_a, total_b], axis=1) + down_bias[None, :]).astype(BF)


def solution(mesh):
    fine = Mesh(mesh.devices.reshape(SIZES), AXES)
    row, col = ("y", "zl", "c"), ("x", "zh")
    placed = (
        P(row, col, None),
        P(),
        P(None, col),
        P(None, col),
        P(None, col),
        P(),
        P(),
        P(None, col),
        P(col),
        P(col, None),
        P(),
    )
    return jax.shard_map(
        shards, mesh=fine, in_specs=placed, out_specs=P(row + col, None), check_vma=False
    )
```

```python
import functools
import math

import jax
import jax.numpy as jnp
import numpy as np
from jax import lax
from jax.experimental import pallas as pl
from jax.experimental.pallas import tpu as pltpu
from jax.sharding import Mesh
from jax.sharding import PartitionSpec as P


HEAD_DIM = 80
EPSILON = 1e-06
AXES = ("y", "zl", "c", "x", "zh")
SIZES = (4, 2, 2, 4, 2)
BF = jnp.bfloat16
F32 = jnp.float32
QUERY_BLOCK = 512
LIMIT = 2.0**64


def pairs(move):
    result = []
    for place in np.ndindex(*SIZES):
        there = dict(zip(AXES, place))
        there.update(move(there))
        target = tuple(there[a] % n for a, n in zip(AXES, SIZES))
        result.append(
            (int(np.ravel_multi_index(place, SIZES)), int(np.ravel_multi_index(target, SIZES)))
        )
    return result


def shift(axis, step):
    return pairs(lambda d: {axis: d[axis] + step})


def send(value, perm):
    return lax.ppermute(value, AXES, perm)


def vmem():
    return pl.BlockSpec(memory_space=pltpu.VMEM)


def smem():
    return pl.BlockSpec(memory_space=pltpu.SMEM)


def call(kernel, outs, ins, scratch=(), flops=0, nbytes=0, exps=0):
    specs = [smem() if k == "s" else vmem() for k, _ in ins]
    return pl.pallas_call(
        kernel,
        out_shape=outs,
        in_specs=specs,
        out_specs=jax.tree.map(lambda _: vmem(), outs),
        scratch_shapes=list(scratch),
        cost_estimate=pl.CostEstimate(flops=flops, bytes_accessed=nbytes, transcendentals=exps),
        compiler_params=pltpu.CompilerParams(vmem_limit_bytes=58 * 2**20),
    )(*[a for _, a in ins])


def norm(values, gain):
    center = values - jnp.mean(values, axis=-1, keepdims=True)
    spread = jnp.mean(center * center, axis=-1, keepdims=True)
    return center * lax.rsqrt(spread + EPSILON) * gain


def project_kernel(c_ref, *refs):
    tiles, rest = refs[:9], refs[9:]
    gain_ref, wq, wk, wv, cos_ref, sin_ref, q_out, kv_out, other_out = rest
    mine = pl.multiple_of(c_ref[0] * HEAD_DIM, 16)
    others = pl.multiple_of((1 - c_ref[0]) * HEAD_DIM, 16)
    weight = jnp.concatenate(
        [w[pl.ds(o, HEAD_DIM), :] for o in (mine, others) for w in (wq, wk, wv)], axis=0
    )
    half = HEAD_DIM // 2
    scale = math.log2(math.e) / math.sqrt(HEAD_DIM)
    groups = [tiles[0:2], tiles[2:4], tiles[4:6], tiles[6:9]]
    for g, group in enumerate(groups):
        rows = jnp.concatenate([t[...] for t in group], axis=0).astype(F32)
        rows = norm(rows, gain_ref[...]).astype(BF)
        mapped = lax.dot_general(
            weight, rows, (((1,), (1,)), ((), ())), preferred_element_type=F32
        )
        at = slice(g * 256, (g + 1) * 256)
        cos, sin = cos_ref[:, at], sin_ref[:, at]

        def turn(u):
            first, second = u[:half], u[half:]
            return jnp.concatenate([first * cos - second * sin, second * cos + first * sin], axis=0)

        part = [mapped[k * HEAD_DIM : (k + 1) * HEAD_DIM] for k in range(6)]
        q_out[:, at] = (turn(part[0]) * scale).astype(BF)
        kv_out[:HEAD_DIM, at] = turn(part[1]).astype(BF)
        kv_out[HEAD_DIM:, at] = part[2].astype(BF)
        other_out[:HEAD_DIM, at] = (turn(part[3]) * scale).astype(BF)
        other_out[HEAD_DIM : 2 * HEAD_DIM, at] = turn(part[4]).astype(BF)
        other_out[2 * HEAD_DIM :, at] = part[5].astype(BF)


def split_rows(m):
    hi = m.astype(BF)
    rest = m - hi.astype(F32)
    mid = rest.astype(BF)
    low = (rest - mid.astype(F32)).astype(BF)
    pad = jnp.zeros((13, m.shape[1]), BF)
    return jnp.concatenate([-hi, -mid, -low, pad], axis=0)


def attend_chunks(chunks, q_ref, m_ref, o_ref, k_all, v_all, flag):
    keys = k_all.shape[0]
    queries = q_ref.shape[1]
    step = keys if keys <= 2048 else max(d for d in (2048, 1536, 1024) if keys % d == 0)
    turns = queries // (2 * QUERY_BLOCK)
    at = 0
    for ref in chunks:
        n = ref.shape[1]
        ones = jnp.ones((16, n), BF)
        k_all[at : at + n, :] = jnp.concatenate([ref[-2 * HEAD_DIM : -HEAD_DIM, :], ones], axis=0).T
        v_all[:, at : at + n] = jnp.concatenate([ref[-HEAD_DIM:, :], ones], axis=0)
        at += n
    flag[0] = 1

    def attempt(tries, carry):
        @pl.when(flag[0] == 1)
        def _():
            o_ref[...] = jnp.zeros_like(o_ref)

            def block(t, carry):
                rows = pl.ds(pl.multiple_of((t // turns) * step, step), step)
                for i in range(2):
                    col = (t % turns) * (2 * QUERY_BLOCK) + i * QUERY_BLOCK
                    cols = pl.ds(pl.multiple_of(col, QUERY_BLOCK), QUERY_BLOCK)
                    s = jnp.dot(k_all[rows, :], q_ref[:, cols], preferred_element_type=F32)
                    p = jnp.exp2(s).astype(BF)
                    o_ref[:, cols] += jnp.dot(v_all[:, rows], p, preferred_element_type=F32)
                return carry

            lax.fori_loop(0, keys // step * turns, block, 0)
            mass = o_ref[HEAD_DIM : HEAD_DIM + 8, :]
            bad = jnp.max(jnp.where(mass < LIMIT, 0.0, 1.0)) > 0.0
            flag[0] = jnp.where(jnp.logical_and(bad, tries == 0), 1, 0)

            @pl.when(flag[0] == 1)
            def _():
                m_ref[1:2, :] = jnp.zeros((1, queries), F32)

                def top_block(t, carry):
                    rows = pl.ds(pl.multiple_of((t // 8) * 512, 512), 512)
                    cols = pl.ds(pl.multiple_of((t % 8) * 256, 256), 256)
                    s = jnp.dot(k_all[rows, :], q_ref[:, cols], preferred_element_type=F32)
                    m_ref[1:2, cols] = jnp.maximum(
                        m_ref[1:2, cols], jnp.max(s, axis=0, keepdims=True)
                    )
                    return carry

                lax.fori_loop(0, keys // 512 * (queries // 256), top_block, 0)
                fresh = m_ref[0:1, :] + m_ref[1:2, :]
                m_ref[0:1, :] = fresh
                q_ref[HEAD_DIM:, :] = split_rows(fresh)

        return carry

    lax.fori_loop(0, 2, attempt, 0)


def first_kernel(own_q, swapped, kv_ref, q_out, start_out, m_ref, o_ref, q_ref, k_all, v_all, flag):
    n = own_q.shape[1]
    q_ref[:HEAD_DIM, :n] = own_q[...]
    q_ref[:HEAD_DIM, n:] = swapped[:HEAD_DIM, :]
    some = kv_ref[:HEAD_DIM, :512].T

    def start(i, carry):
        cols = pl.ds(pl.multiple_of(i * QUERY_BLOCK, QUERY_BLOCK), QUERY_BLOCK)
        s = jnp.dot(some, q_ref[:HEAD_DIM, cols], preferred_element_type=F32)
        m_ref[:, cols] = jnp.broadcast_to(jnp.max(s, axis=0, keepdims=True), (8, QUERY_BLOCK))
        return carry

    lax.fori_loop(0, 2 * n // QUERY_BLOCK, start, 0)
    q_ref[HEAD_DIM:, :] = split_rows(m_ref[0:1, :])
    q_out[...] = q_ref[...]
    start_out[...] = m_ref[...]
    attend_chunks([kv_ref], q_ref, m_ref, o_ref, k_all, v_all, flag)


def next_kernel(count, *refs):
    chunks, rest = refs[:count], refs[count:]
    q_in, m_in, m_ref, o_ref, q_ref, k_all, v_all, flag = rest
    q_ref[...] = q_in[...]
    m_ref[...] = m_in[...]
    attend_chunks(chunks, q_ref, m_ref, o_ref, k_all, v_all, flag)


def last_kernel(count, done, place, *refs):
    chunks, rest = refs[:count], refs[count:]
    q_in, m_in = rest[:2]
    tops, sums = rest[2 : 2 + done], rest[2 + done : 2 + 2 * done]
    own_ref, swap_ref, q_ref, m_ref, o_ref, k_all, v_all, flag = rest[2 + 2 * done :]
    q_ref[...] = q_in[...]
    m_ref[...] = m_in[...]
    attend_chunks(chunks, q_ref, m_ref, o_ref, k_all, v_all, flag)
    top = m_ref[0:1, :]
    for t in tops:
        top = jnp.maximum(top, t[0:1, :])
    total = o_ref[...] * jnp.exp2(m_ref[0:1, :] - top)
    for t, o in zip(tops, sums):
        total = total + o[...] * jnp.exp2(t[0:1, :] - top)
    half = total.shape[1] // 2
    for out_ref, lower in ((own_ref, 0), (swap_ref, half)):
        for s in range(half // 128):
            cols = slice(lower + s * 128, lower + (s + 1) * 128)
            mass = total[HEAD_DIM : HEAD_DIM + 1, cols]
            target = pl.ds(pl.multiple_of(place[s] * 128, 128), 128)
            out_ref[:, target] = (total[:HEAD_DIM, cols] / mass).astype(BF)


def merge_kernel(col_ref, c_ref, *refs):
    pieces, tiles, rest = refs[:9], refs[9:18], refs[18:]
    out_weight, gain_ref, up_weight, bias_ref = rest[:4]
    hidden_a, hidden_b, att_all, token_all, mixed_all, merged = rest[4:]
    starts = [0, 0, 0, 0, 0, 0, 0, 0, 80]
    slots = [0, 1, 2, 3, 4, 5, 6, 7, 7]
    c, x, zh = c_ref[0], c_ref[1], c_ref[2]
    for piece, tile, slot, lower in zip(pieces, tiles, slots, starts):
        for part in range(piece.shape[0] // 80):
            odd = (lower + part * 80) // 80
            spot = col_ref[slot] * 160 + (c if odd == 0 else 1 - c) * 80
            att_all[pl.ds(pl.multiple_of(spot, 16), 80), :] = piece[part * 80 : (part + 1) * 80, :]
        row = slot * 128 + (64 if lower else 0)
        token_all[row : row + tile.shape[0], :] = tile[...]
    width = out_weight.shape[1]

    def project(i, carry):
        spot = pl.ds(pl.multiple_of(i * 256, 256), 256)
        lhs = att_all[:, spot].T
        mixed_all[spot, :] = jnp.dot(lhs, out_weight[...], preferred_element_type=F32)
        return carry

    lax.fori_loop(0, 4, project, 0)
    r = lax.broadcasted_iota(jnp.int32, (128, 128), 0)
    t = lax.broadcasted_iota(jnp.int32, (128, 128), 1)
    a, b, u, w = r >> 6, (r >> 5) & 1, (r >> 3) & 3, r & 7
    pick = ((2 * u + a) * 16 + 2 * w + b == t).astype(BF)

    def settle(s, carry):
        spot = pl.ds(pl.multiple_of(col_ref[s] * 128, 128), 128)
        own = pl.ds(pl.multiple_of(s * 128, 128), 128)
        residual = token_all[own, :].astype(F32) + mixed_all[spot, :]
        normed = norm(residual, gain_ref[...]).astype(BF)
        ordered = jnp.dot(pick, normed, preferred_element_type=F32).astype(BF)
        for q in range(4):
            merged[q, pl.ds(pl.multiple_of(s * 32, 32), 32), :] = ordered[q * 32 : (q + 1) * 32]
        return carry

    lax.fori_loop(0, 8, settle, 0)
    z = bias_ref[...]
    for q in range(4):
        z = z + jnp.dot(
            merged[q], up_weight[q * width : (q + 1) * width, :], preferred_element_type=F32
        )
    hidden = (0.5 * z * (1.0 + lax.erf(z * (1.0 / math.sqrt(2.0))))).astype(BF)
    n = hidden.shape[0]
    rows = lax.broadcasted_iota(jnp.int32, (n, n), 0)
    lane = lax.broadcasted_iota(jnp.int32, (1, n), 1)
    col = jnp.zeros((1, n), jnp.int32)
    for s in range(8):
        col = jnp.where((lane >> 5) == s, col_ref[s], col)
    raster = ((lane >> 3) & 3) * 64 + col * 8 + (lane & 7)
    owner = raster >> 5
    ahead = ((owner >> 1) - x) & 3
    other_half = (owner & 1) ^ zh
    place_a = ahead * 64 + other_half * 32 + (raster & 31)
    place_b = other_half * 128 + ahead * 32 + (raster & 31)
    for place, out in ((place_a, hidden_a), (place_b, hidden_b)):
        out[...] = jnp.dot(
            (rows == place).astype(BF), hidden, preferred_element_type=F32
        ).astype(BF)


def spread(own, axis, across, dim, extras=()):
    forward, backward = shift(axis, 1), shift(axis, -1)
    half = own.shape[dim] // 2
    plus, minus, mirror = send(own, forward), send(own, backward), send(own, across)
    plus, minus, mirror, extras = lax.optimization_barrier((plus, minus, mirror, extras))
    two = send(plus, forward)
    mirror_plus = send(plus, across)
    mirror_minus = send(mirror, backward)
    far_low = send(lax.slice_in_dim(mirror_plus, 0, half, axis=dim), forward)
    far_high = send(lax.slice_in_dim(two, half, 2 * half, axis=dim), across)
    return [own, plus, minus, mirror, two, mirror_plus, mirror_minus, far_low, far_high], extras


def shards(
    patches,
    norm_gain,
    query_weight,
    key_weight,
    value_weight,
    out_weight,
    merge_gain,
    up_weight,
    up_bias,
    down_weight,
    down_bias,
):
    band_height, tile_width, model_width = patches.shape
    tile = band_height * tile_width
    band = tile * 8
    y, zl, c = lax.axis_index("y"), lax.axis_index("zl"), lax.axis_index("c")
    x, zh = lax.axis_index("x"), lax.axis_index("zh")
    row_index = (y * 2 + zl) * 2 + c
    sds = jax.ShapeDtypeStruct

    slot_x = jnp.stack([x, x - 1, x + 1, x, x + 2, x - 1, x + 1, x + 2]) % 4
    slot_z = jnp.stack([zh, zh, zh, 1 - zh, zh, 1 - zh, 1 - zh, 1 - zh])
    slot_col = (slot_x * 2 + slot_z).astype(jnp.int32)
    local = np.arange(tile)
    row_coord = (row_index * band_height + jnp.tile(local // tile_width, 8)).astype(F32)
    col_coord = (
        (slot_col[:, None] * tile_width + (local % tile_width)[None, :]).astype(F32).reshape(-1)
    )
    frequency = 1.0 / 10000.0 ** (
        jnp.arange(HEAD_DIM // 4, dtype=F32) * 2.0 / (HEAD_DIM // 2)
    )
    angles = jnp.concatenate(
        [frequency[:, None] * row_coord[None, :], frequency[:, None] * col_coord[None, :]], axis=0
    )
    cos, sin = jnp.cos(angles), jnp.sin(angles)

    mirror_x = pairs(lambda d: {"zh": 1 - d["zh"]})
    tokens = patches.reshape(tile, model_width)
    gains = [v.reshape(1, -1) for v in (norm_gain, merge_gain, up_bias)]
    tiles, (cos, sin, gains) = spread(tokens, "x", mirror_x, 0, (cos, sin, gains))
    q_own, kv_own, other = call(
        project_kernel,
        (sds((HEAD_DIM, band), BF), sds((2 * HEAD_DIM, band), BF), sds((3 * HEAD_DIM, band), BF)),
        [("s", c.reshape(1).astype(jnp.int32))]
        + [("v", t) for t in tiles]
        + [("v", gains[0])]
        + [("v", query_weight.T), ("v", key_weight.T), ("v", value_weight.T), ("v", cos), ("v", sin)],
        flops=2 * band * model_width * 480,
    )
    n = 2 * band
    swap = pairs(lambda d: {"c": 1 - d["c"]})
    mirror_y = pairs(lambda d: {"zl": 1 - d["zl"]})
    swapped = send(other, swap)
    kv = jnp.concatenate([kv_own, swapped[HEAD_DIM:]], axis=1)
    chunks, _ = spread(kv, "y", mirror_y, 1)
    groups = (chunks[1:4], chunks[4:7], chunks[7:])
    q_shape, m_shape, o_shape = sds((96, n), BF), sds((8, n), F32), sds((96, n), F32)

    def scratch(keys):
        return [
            pltpu.VMEM((96, n), BF),
            pltpu.VMEM((keys, 96), BF),
            pltpu.VMEM((96, keys), BF),
            pltpu.SMEM((1,), jnp.int32),
        ]

    work = lambda keys: dict(flops=2 * n * keys * 512, exps=n * keys, nbytes=4 * n * 96)
    q, start, top, part = call(
        first_kernel,
        (q_shape, m_shape, m_shape, o_shape),
        [("v", q_own), ("v", swapped), ("v", kv)],
        scratch(n),
        **work(n),
    )
    tops, parts = [top], [part]
    for chunks in groups[:-1]:
        keys = sum(t.shape[1] for t in chunks)
        top, part = call(
            functools.partial(next_kernel, len(chunks)),
            (m_shape, o_shape),
            [("v", t) for t in chunks] + [("v", q), ("v", start)],
            scratch(keys),
            **work(keys),
        )
        tops.append(top)
        parts.append(part)
    final = scratch(n)
    half_shape = sds((HEAD_DIM, band), BF)
    attended, partner = call(
        functools.partial(last_kernel, 2, len(tops)),
        (half_shape, half_shape),
        [("s", slot_col)] + [("v", t) for t in (*groups[-1], q, start, *tops, *parts)],
        [final[0], pltpu.VMEM((8, n), F32), pltpu.VMEM((96, n), F32), *final[1:]],
        **work(n),
    )
    attended = jnp.concatenate([attended, send(partner, swap)], axis=0)
    pieces, _ = spread(attended, "x", mirror_x, 0)
    hidden_a, hidden_b = call(
        merge_kernel,
        (sds((256, up_weight.shape[1]), BF),) * 2,
        [("s", slot_col), ("s", jnp.stack([c, x, zh]).astype(jnp.int32))]
        + [("v", t) for t in (*pieces, *tiles)]
        + [
            ("v", out_weight),
            ("v", gains[1]),
            ("v", up_weight),
            ("v", gains[2]),
        ],
        [
            pltpu.VMEM((model_width, band), BF),
            pltpu.VMEM((band, model_width), BF),
            pltpu.VMEM((band, model_width), F32),
            pltpu.VMEM((4, 256, model_width), BF),
        ],
        flops=2 * 256 * 5120 * 640 + 2 * band * model_width * model_width,
    )
    return scatter_output(hidden_a, hidden_b, down_weight, down_bias, mirror_x)


def ring(block, rows):
    forward, backward = shift("x", 1), shift("x", -1)
    half = block.shape[1] // 2
    part = lambda k: block[k * rows : (k + 1) * rows]
    ahead, behind, far = part(1), part(3), part(2)
    from_behind = send(far[:, :half], forward)
    from_ahead = send(far[:, half:], backward)
    add = lambda p, q: (p.astype(F32) + q.astype(F32)).astype(BF)
    onward = jnp.concatenate([add(ahead[:, :half], from_behind), ahead[:, half:]], axis=1)
    back = jnp.concatenate([behind[:, :half], add(behind[:, half:], from_ahead)], axis=1)
    got_behind, got_ahead = send(onward, forward), send(back, backward)
    return part(0).astype(F32) + got_behind.astype(F32) + got_ahead.astype(F32)


def scatter_output(hidden_a, hidden_b, down_weight, down_bias, mirror):
    split = 4608
    part_b = jnp.dot(
        hidden_b, down_weight[:, split:], preferred_element_type=F32
    ).astype(BF)
    give_b, hidden_a = lax.optimization_barrier((part_b[128:], hidden_a))
    got_b = send(give_b, mirror)
    part_a = jnp.dot(
        hidden_a, down_weight[:, :split], preferred_element_type=F32
    ).astype(BF)
    total_a = ring(part_a, 64)
    got_a = send(total_a[32:].astype(BF), mirror)
    block_b = (part_b[:128].astype(F32) + got_b.astype(F32)).astype(BF)
    total_b = ring(block_b, 32)
    total_a = total_a[:32] + got_a.astype(F32)
    return (jnp.concatenate([total_a, total_b], axis=1) + down_bias[None, :]).astype(BF)


def solution(mesh):
    fine = Mesh(mesh.devices.reshape(SIZES), AXES)
    row, col = ("y", "zl", "c"), ("x", "zh")
    placed = (
        P(row, col, None),
        P(),
        P(None, col),
        P(None, col),
        P(None, col),
        P(),
        P(),
        P(None, col),
        P(col),
        P(col, None),
        P(),
    )

    return jax.shard_map(
        shards, mesh=fine, in_specs=placed, out_specs=P(row + col, None), check_vma=False
    )
```

```python
import functools
import math

import jax
import jax.numpy as jnp
import numpy as np
from jax import lax
from jax.experimental import pallas as pl
from jax.experimental.pallas import tpu as pltpu
from jax.sharding import Mesh
from jax.sharding import PartitionSpec as P


HEAD_DIM = 80
EPSILON = 1e-06
AXES = ("y", "zl", "c", "x", "zh")
SIZES = (4, 2, 2, 4, 2)
BF = jnp.bfloat16
F32 = jnp.float32
QUERY_BLOCK = 512
LIMIT = 2.0**64


def pairs(move):
    result = []
    for place in np.ndindex(*SIZES):
        there = dict(zip(AXES, place))
        there.update(move(there))
        target = tuple(there[a] % n for a, n in zip(AXES, SIZES))
        result.append(
            (int(np.ravel_multi_index(place, SIZES)), int(np.ravel_multi_index(target, SIZES)))
        )
    return result


def shift(axis, step):
    return pairs(lambda d: {axis: d[axis] + step})


def send(value, perm):
    return lax.ppermute(value, AXES, perm)


def vmem():
    return pl.BlockSpec(memory_space=pltpu.VMEM)


def smem():
    return pl.BlockSpec(memory_space=pltpu.SMEM)


def call(kernel, outs, ins, scratch=(), flops=0, nbytes=0, exps=0, grant=8):
    specs = [smem() if k == "s" else vmem() for k, _ in ins]
    return pl.pallas_call(
        kernel,
        out_shape=outs,
        in_specs=specs,
        out_specs=jax.tree.map(lambda _: vmem(), outs),
        scratch_shapes=list(scratch),
        cost_estimate=pl.CostEstimate(flops=flops, bytes_accessed=nbytes, transcendentals=exps),
        compiler_params=pltpu.CompilerParams(vmem_limit_bytes=grant * 2**20),
    )(*[a for _, a in ins])


def norm(values, gain):
    center = values - jnp.mean(values, axis=-1, keepdims=True)
    spread = jnp.mean(center * center, axis=-1, keepdims=True)
    return center * lax.rsqrt(spread + EPSILON) * gain


def project_kernel(c_ref, *refs):
    tiles, rest = refs[:9], refs[9:]
    gain_ref, wq, wk, wv, cos_ref, sin_ref, q_out, kv_out, other_out = rest
    mine = pl.multiple_of(c_ref[0] * HEAD_DIM, 16)
    others = pl.multiple_of((1 - c_ref[0]) * HEAD_DIM, 16)
    weight = jnp.concatenate(
        [w[pl.ds(o, HEAD_DIM), :] for o in (mine, others) for w in (wq, wk, wv)], axis=0
    )
    half = HEAD_DIM // 2
    scale = math.log2(math.e) / math.sqrt(HEAD_DIM)
    groups = [tiles[0:2], tiles[2:4], tiles[4:6], tiles[6:9]]
    for g, group in enumerate(groups):
        rows = jnp.concatenate([t[...] for t in group], axis=0).astype(F32)
        rows = norm(rows, gain_ref[...]).astype(BF)
        mapped = lax.dot_general(
            weight, rows, (((1,), (1,)), ((), ())), preferred_element_type=F32
        )
        at = slice(g * 256, (g + 1) * 256)
        cos, sin = cos_ref[:, at], sin_ref[:, at]

        def turn(u):
            first, second = u[:half], u[half:]
            return jnp.concatenate([first * cos - second * sin, second * cos + first * sin], axis=0)

        part = [mapped[k * HEAD_DIM : (k + 1) * HEAD_DIM] for k in range(6)]
        q_out[:, at] = (turn(part[0]) * scale).astype(BF)
        kv_out[:HEAD_DIM, at] = turn(part[1]).astype(BF)
        kv_out[HEAD_DIM:, at] = part[2].astype(BF)
        other_out[:HEAD_DIM, at] = (turn(part[3]) * scale).astype(BF)
        other_out[HEAD_DIM : 2 * HEAD_DIM, at] = turn(part[4]).astype(BF)
        other_out[2 * HEAD_DIM :, at] = part[5].astype(BF)


def split_rows(m):
    hi = m.astype(BF)
    rest = m - hi.astype(F32)
    mid = rest.astype(BF)
    low = (rest - mid.astype(F32)).astype(BF)
    pad = jnp.zeros((13, m.shape[1]), BF)
    return jnp.concatenate([-hi, -mid, -low, pad], axis=0)


def attend_chunks(chunks, q_ref, m_ref, o_ref, k_all, v_all, flag):
    keys = k_all.shape[0]
    queries = q_ref.shape[1]
    step = keys if keys <= 2048 else max(d for d in (2048, 1536, 1024) if keys % d == 0)
    turns = queries // (2 * QUERY_BLOCK)
    at = 0
    for ref in chunks:
        n = ref.shape[1]
        ones = jnp.ones((16, n), BF)
        k_all[at : at + n, :] = jnp.concatenate([ref[-2 * HEAD_DIM : -HEAD_DIM, :], ones], axis=0).T
        v_all[:, at : at + n] = jnp.concatenate([ref[-HEAD_DIM:, :], ones], axis=0)
        at += n
    flag[0] = 1

    def attempt(tries, carry):
        @pl.when(flag[0] == 1)
        def _():
            o_ref[...] = jnp.zeros_like(o_ref)

            def block(t, carry):
                rows = pl.ds(pl.multiple_of((t // turns) * step, step), step)
                for i in range(2):
                    col = (t % turns) * (2 * QUERY_BLOCK) + i * QUERY_BLOCK
                    cols = pl.ds(pl.multiple_of(col, QUERY_BLOCK), QUERY_BLOCK)
                    s = jnp.dot(k_all[rows, :], q_ref[:, cols], preferred_element_type=F32)
                    p = jnp.exp2(s).astype(BF)
                    o_ref[:, cols] += jnp.dot(v_all[:, rows], p, preferred_element_type=F32)
                return carry

            lax.fori_loop(0, keys // step * turns, block, 0)
            mass = o_ref[HEAD_DIM : HEAD_DIM + 8, :]
            bad = jnp.max(jnp.where(mass < LIMIT, 0.0, 1.0)) > 0.0
            flag[0] = jnp.where(jnp.logical_and(bad, tries == 0), 1, 0)

            @pl.when(flag[0] == 1)
            def _():
                m_ref[1:2, :] = jnp.zeros((1, queries), F32)

                def top_block(t, carry):
                    rows = pl.ds(pl.multiple_of((t // 8) * 512, 512), 512)
                    cols = pl.ds(pl.multiple_of((t % 8) * 256, 256), 256)
                    s = jnp.dot(k_all[rows, :], q_ref[:, cols], preferred_element_type=F32)
                    m_ref[1:2, cols] = jnp.maximum(
                        m_ref[1:2, cols], jnp.max(s, axis=0, keepdims=True)
                    )
                    return carry

                lax.fori_loop(0, keys // 512 * (queries // 256), top_block, 0)
                fresh = m_ref[0:1, :] + m_ref[1:2, :]
                m_ref[0:1, :] = fresh
                q_ref[HEAD_DIM:, :] = split_rows(fresh)

        return carry

    lax.fori_loop(0, 2, attempt, 0)


def first_kernel(own_q, swapped, kv_ref, q_out, start_out, m_ref, o_ref, q_ref, k_all, v_all, flag):
    n = own_q.shape[1]
    q_ref[:HEAD_DIM, :n] = own_q[...]
    q_ref[:HEAD_DIM, n:] = swapped[:HEAD_DIM, :]
    some = kv_ref[:HEAD_DIM, :512].T

    def start(i, carry):
        cols = pl.ds(pl.multiple_of(i * QUERY_BLOCK, QUERY_BLOCK), QUERY_BLOCK)
        s = jnp.dot(some, q_ref[:HEAD_DIM, cols], preferred_element_type=F32)
        m_ref[:, cols] = jnp.broadcast_to(jnp.max(s, axis=0, keepdims=True), (8, QUERY_BLOCK))
        return carry

    lax.fori_loop(0, 2 * n // QUERY_BLOCK, start, 0)
    q_ref[HEAD_DIM:, :] = split_rows(m_ref[0:1, :])
    q_out[...] = q_ref[...]
    start_out[...] = m_ref[...]
    attend_chunks([kv_ref], q_ref, m_ref, o_ref, k_all, v_all, flag)


def next_kernel(count, *refs):
    chunks, rest = refs[:count], refs[count:]
    q_in, m_in, m_ref, o_ref, q_ref, k_all, v_all, flag = rest
    q_ref[...] = q_in[...]
    m_ref[...] = m_in[...]
    attend_chunks(chunks, q_ref, m_ref, o_ref, k_all, v_all, flag)


def last_kernel(count, done, place, *refs):
    chunks, rest = refs[:count], refs[count:]
    q_in, m_in = rest[:2]
    tops, sums = rest[2 : 2 + done], rest[2 + done : 2 + 2 * done]
    own_ref, swap_ref, q_ref, m_ref, o_ref, k_all, v_all, flag = rest[2 + 2 * done :]
    q_ref[...] = q_in[...]
    m_ref[...] = m_in[...]
    attend_chunks(chunks, q_ref, m_ref, o_ref, k_all, v_all, flag)
    top = m_ref[0:1, :]
    for t in tops:
        top = jnp.maximum(top, t[0:1, :])
    total = o_ref[...] * jnp.exp2(m_ref[0:1, :] - top)
    for t, o in zip(tops, sums):
        total = total + o[...] * jnp.exp2(t[0:1, :] - top)
    half = total.shape[1] // 2
    for out_ref, lower in ((own_ref, 0), (swap_ref, half)):
        for s in range(half // 128):
            cols = slice(lower + s * 128, lower + (s + 1) * 128)
            mass = total[HEAD_DIM : HEAD_DIM + 1, cols]
            target = pl.ds(pl.multiple_of(place[s] * 128, 128), 128)
            out_ref[:, target] = (total[:HEAD_DIM, cols] / mass).astype(BF)


def merge_kernel(col_ref, c_ref, *refs):
    pieces, tiles, rest = refs[:9], refs[9:18], refs[18:]
    out_weight, gain_ref, up_weight, bias_ref = rest[:4]
    hidden_a, hidden_b, att_all, token_all, mixed_all, merged = rest[4:]
    starts = [0, 0, 0, 0, 0, 0, 0, 0, 80]
    slots = [0, 1, 2, 3, 4, 5, 6, 7, 7]
    c, x, zh = c_ref[0], c_ref[1], c_ref[2]
    for piece, tile, slot, lower in zip(pieces, tiles, slots, starts):
        for part in range(piece.shape[0] // 80):
            odd = (lower + part * 80) // 80
            spot = col_ref[slot] * 160 + (c if odd == 0 else 1 - c) * 80
            att_all[pl.ds(pl.multiple_of(spot, 16), 80), :] = piece[part * 80 : (part + 1) * 80, :]
        row = slot * 128 + (64 if lower else 0)
        token_all[row : row + tile.shape[0], :] = tile[...]
    width = out_weight.shape[1]

    def project(i, carry):
        spot = pl.ds(pl.multiple_of(i * 512, 512), 512)
        lhs = att_all[:, spot].T
        mixed_all[spot, :] = jnp.dot(lhs, out_weight[...], preferred_element_type=F32)
        return carry

    lax.fori_loop(0, 2, project, 0)
    r = lax.broadcasted_iota(jnp.int32, (128, 128), 0)
    t = lax.broadcasted_iota(jnp.int32, (128, 128), 1)
    a, b, u, w = r >> 6, (r >> 5) & 1, (r >> 3) & 3, r & 7
    pick = ((2 * u + a) * 16 + 2 * w + b == t).astype(BF)

    def settle(turn, carry):
        for k in range(4):
            s = turn * 4 + k
            spot = pl.ds(pl.multiple_of(col_ref[s] * 128, 128), 128)
            own = pl.ds(pl.multiple_of(s * 128, 128), 128)
            residual = token_all[own, :].astype(F32) + mixed_all[spot, :]
            normed = norm(residual, gain_ref[...]).astype(BF)
            ordered = jnp.dot(pick, normed, preferred_element_type=F32).astype(BF)
            rows = pl.ds(pl.multiple_of(s * 32, 32), 32)
            for q in range(4):
                merged[q, rows, :] = ordered[q * 32 : (q + 1) * 32]
        return carry

    lax.fori_loop(0, 2, settle, 0)
    z = bias_ref[...]
    for q in range(4):
        z = z + jnp.dot(
            merged[q], up_weight[q * width : (q + 1) * width, :], preferred_element_type=F32
        )
    hidden = (0.5 * z * (1.0 + lax.erf(z * (1.0 / math.sqrt(2.0))))).astype(BF)
    n = hidden.shape[0]
    rows = lax.broadcasted_iota(jnp.int32, (n, n), 0)
    lane = lax.broadcasted_iota(jnp.int32, (1, n), 1)
    col = jnp.zeros((1, n), jnp.int32)
    for s in range(8):
        col = jnp.where((lane >> 5) == s, col_ref[s], col)
    raster = ((lane >> 3) & 3) * 64 + col * 8 + (lane & 7)
    owner = raster >> 5
    ahead = ((owner >> 1) - x) & 3
    other_half = (owner & 1) ^ zh
    place_a = ahead * 64 + other_half * 32 + (raster & 31)
    place_b = other_half * 128 + ahead * 32 + (raster & 31)
    for place, out in ((place_a, hidden_a), (place_b, hidden_b)):
        out[...] = jnp.dot(
            (rows == place).astype(BF), hidden, preferred_element_type=F32
        ).astype(BF)


def spread(own, axis, across, dim, extras=()):
    forward, backward = shift(axis, 1), shift(axis, -1)
    half = own.shape[dim] // 2
    plus, minus, mirror = send(own, forward), send(own, backward), send(own, across)
    plus, minus, mirror, extras = lax.optimization_barrier((plus, minus, mirror, extras))
    two = send(plus, forward)
    mirror_plus = send(plus, across)
    mirror_minus = send(mirror, backward)
    far_low = send(lax.slice_in_dim(mirror_plus, 0, half, axis=dim), forward)
    far_high = send(lax.slice_in_dim(two, half, 2 * half, axis=dim), across)
    return [own, plus, minus, mirror, two, mirror_plus, mirror_minus, far_low, far_high], extras


def shards(
    patches,
    norm_gain,
    query_weight,
    key_weight,
    value_weight,
    out_weight,
    merge_gain,
    up_weight,
    up_bias,
    down_weight,
    down_bias,
):
    band_height, tile_width, model_width = patches.shape
    tile = band_height * tile_width
    band = tile * 8
    y, zl, c = lax.axis_index("y"), lax.axis_index("zl"), lax.axis_index("c")
    x, zh = lax.axis_index("x"), lax.axis_index("zh")
    row_index = (y * 2 + zl) * 2 + c
    sds = jax.ShapeDtypeStruct

    slot_x = jnp.stack([x, x - 1, x + 1, x, x + 2, x - 1, x + 1, x + 2]) % 4
    slot_z = jnp.stack([zh, zh, zh, 1 - zh, zh, 1 - zh, 1 - zh, 1 - zh])
    slot_col = (slot_x * 2 + slot_z).astype(jnp.int32)
    local = np.arange(tile)
    row_coord = (row_index * band_height + jnp.tile(local // tile_width, 8)).astype(F32)
    col_coord = (
        (slot_col[:, None] * tile_width + (local % tile_width)[None, :]).astype(F32).reshape(-1)
    )
    frequency = 1.0 / 10000.0 ** (
        jnp.arange(HEAD_DIM // 4, dtype=F32) * 2.0 / (HEAD_DIM // 2)
    )
    angles = jnp.concatenate(
        [frequency[:, None] * row_coord[None, :], frequency[:, None] * col_coord[None, :]], axis=0
    )
    cos, sin = jnp.cos(angles), jnp.sin(angles)

    mirror_x = pairs(lambda d: {"zh": 1 - d["zh"]})
    tokens = patches.reshape(tile, model_width)
    gains = [v.reshape(1, -1) for v in (norm_gain, merge_gain, up_bias)]
    tiles, (cos, sin, gains) = spread(tokens, "x", mirror_x, 0, (cos, sin, gains))
    q_own, kv_own, other = call(
        project_kernel,
        (sds((HEAD_DIM, band), BF), sds((2 * HEAD_DIM, band), BF), sds((3 * HEAD_DIM, band), BF)),
        [("s", c.reshape(1).astype(jnp.int32))]
        + [("v", t) for t in tiles]
        + [("v", gains[0])]
        + [("v", query_weight.T), ("v", key_weight.T), ("v", value_weight.T), ("v", cos), ("v", sin)],
        flops=2 * band * model_width * 480,
    )
    n = 2 * band
    swap = pairs(lambda d: {"c": 1 - d["c"]})
    mirror_y = pairs(lambda d: {"zl": 1 - d["zl"]})
    swapped = send(other, swap)
    kv = jnp.concatenate([kv_own, swapped[HEAD_DIM:]], axis=1)
    chunks, _ = spread(kv, "y", mirror_y, 1)
    groups = (chunks[1:4], chunks[4:7], chunks[7:])
    q_shape, m_shape, o_shape = sds((96, n), BF), sds((8, n), F32), sds((96, n), F32)

    def scratch(keys):
        return [
            pltpu.VMEM((96, n), BF),
            pltpu.VMEM((keys, 96), BF),
            pltpu.VMEM((96, keys), BF),
            pltpu.SMEM((1,), jnp.int32),
        ]

    work = lambda keys: dict(flops=2 * n * keys * 512, exps=n * keys, nbytes=4 * n * 96)
    q, start, top, part = call(
        first_kernel,
        (q_shape, m_shape, m_shape, o_shape),
        [("v", q_own), ("v", swapped), ("v", kv)],
        scratch(n),
        **work(n),
    )
    tops, parts = [top], [part]
    for chunks in groups[:-1]:
        keys = sum(t.shape[1] for t in chunks)
        top, part = call(
            functools.partial(next_kernel, len(chunks)),
            (m_shape, o_shape),
            [("v", t) for t in chunks] + [("v", q), ("v", start)],
            scratch(keys),
            **work(keys),
        )
        tops.append(top)
        parts.append(part)
    final = scratch(n)
    half_shape = sds((HEAD_DIM, band), BF)
    attended, partner = call(
        functools.partial(last_kernel, 2, len(tops)),
        (half_shape, half_shape),
        [("s", slot_col)] + [("v", t) for t in (*groups[-1], q, start, *tops, *parts)],
        [final[0], pltpu.VMEM((8, n), F32), pltpu.VMEM((96, n), F32), *final[1:]],
        **work(n),
    )
    attended = jnp.concatenate([attended, send(partner, swap)], axis=0)
    pieces, _ = spread(attended, "x", mirror_x, 0)
    hidden_a, hidden_b = call(
        merge_kernel,
        (sds((256, up_weight.shape[1]), BF),) * 2,
        [("s", slot_col), ("s", jnp.stack([c, x, zh]).astype(jnp.int32))]
        + [("v", t) for t in (*pieces, *tiles)]
        + [
            ("v", out_weight),
            ("v", gains[1]),
            ("v", up_weight),
            ("v", gains[2]),
        ],
        [
            pltpu.VMEM((model_width, band), BF),
            pltpu.VMEM((band, model_width), BF),
            pltpu.VMEM((band, model_width), F32),
            pltpu.VMEM((4, 256, model_width), BF),
        ],
        flops=2 * 256 * 5120 * 640 + 2 * band * model_width * model_width,
        grant=18,
    )
    return scatter_output(hidden_a, hidden_b, down_weight, down_bias, mirror_x)


def ring(block, rows):
    forward, backward = shift("x", 1), shift("x", -1)
    half = block.shape[1] // 2
    part = lambda k: block[k * rows : (k + 1) * rows]
    ahead, behind, far = part(1), part(3), part(2)
    from_behind = send(far[:, :half], forward)
    from_ahead = send(far[:, half:], backward)
    add = lambda p, q: (p.astype(F32) + q.astype(F32)).astype(BF)
    onward = jnp.concatenate([add(ahead[:, :half], from_behind), ahead[:, half:]], axis=1)
    back = jnp.concatenate([behind[:, :half], add(behind[:, half:], from_ahead)], axis=1)
    got_behind, got_ahead = send(onward, forward), send(back, backward)
    return part(0).astype(F32) + got_behind.astype(F32) + got_ahead.astype(F32)


def scatter_output(hidden_a, hidden_b, down_weight, down_bias, mirror):
    split = 4608
    part_b = jnp.dot(
        hidden_b, down_weight[:, split:], preferred_element_type=F32
    ).astype(BF)
    give_b, hidden_a = lax.optimization_barrier((part_b[128:], hidden_a))
    got_b = send(give_b, mirror)
    part_a = jnp.dot(
        hidden_a, down_weight[:, :split], preferred_element_type=F32
    ).astype(BF)
    total_a = ring(part_a, 64)
    got_a = send(total_a[32:].astype(BF), mirror)
    block_b = (part_b[:128].astype(F32) + got_b.astype(F32)).astype(BF)
    total_b = ring(block_b, 32)
    total_a = total_a[:32] + got_a.astype(F32)
    return (jnp.concatenate([total_a, total_b], axis=1) + down_bias[None, :]).astype(BF)


def solution(mesh):
    fine = Mesh(mesh.devices.reshape(SIZES), AXES)
    row, col = ("y", "zl", "c"), ("x", "zh")
    placed = (
        P(row, col, None),
        P(),
        P(None, col),
        P(None, col),
        P(None, col),
        P(),
        P(),
        P(None, col),
        P(col),
        P(col, None),
        P(),
    )

    return jax.shard_map(
        shards, mesh=fine, in_specs=placed, out_specs=P(row + col, None), check_vma=False
    )
```

```python
import functools
import math

import jax
import jax.numpy as jnp
import numpy as np
from jax import lax
from jax.experimental import pallas as pl
from jax.experimental.pallas import tpu as pltpu
from jax.sharding import Mesh
from jax.sharding import PartitionSpec as P


HEAD_DIM = 80
EPSILON = 1e-06
AXES = ("y", "zl", "c", "x", "zh")
SIZES = (4, 2, 2, 4, 2)
BF = jnp.bfloat16
F32 = jnp.float32
QUERY_BLOCK = 512
LIMIT = 2.0**64


def pairs(move):
    result = []
    for place in np.ndindex(*SIZES):
        there = dict(zip(AXES, place))
        there.update(move(there))
        target = tuple(there[a] % n for a, n in zip(AXES, SIZES))
        result.append(
            (int(np.ravel_multi_index(place, SIZES)), int(np.ravel_multi_index(target, SIZES)))
        )
    return result


def shift(axis, step):
    return pairs(lambda d: {axis: d[axis] + step})


def send(value, perm):
    return lax.ppermute(value, AXES, perm)


def vmem():
    return pl.BlockSpec(memory_space=pltpu.VMEM)


def smem():
    return pl.BlockSpec(memory_space=pltpu.SMEM)


def call(kernel, outs, ins, scratch=(), flops=0, nbytes=0, exps=0, grant=8, alias=None):
    specs = [smem() if k == "s" else vmem() for k, _ in ins]
    return pl.pallas_call(
        kernel,
        out_shape=outs,
        in_specs=specs,
        out_specs=jax.tree.map(lambda _: vmem(), outs),
        scratch_shapes=list(scratch),
        input_output_aliases=alias or {},
        cost_estimate=pl.CostEstimate(flops=flops, bytes_accessed=nbytes, transcendentals=exps),
        compiler_params=pltpu.CompilerParams(vmem_limit_bytes=grant * 2**20),
    )(*[a for _, a in ins])


def norm(values, gain):
    center = values - jnp.mean(values, axis=-1, keepdims=True)
    spread = jnp.mean(center * center, axis=-1, keepdims=True)
    return center * lax.rsqrt(spread + EPSILON) * gain


def project_kernel(groups, at, c_ref, gain_ref, wq, wk, wv, cos_ref, sin_ref, *refs):
    tiles = refs[: sum(groups)]
    q_out, kv_out, other_out = refs[-3:]
    mine = pl.multiple_of(c_ref[0] * HEAD_DIM, 16)
    others = pl.multiple_of((1 - c_ref[0]) * HEAD_DIM, 16)
    weight = jnp.concatenate(
        [w[pl.ds(o, HEAD_DIM), :] for o in (mine, others) for w in (wq, wk, wv)], axis=0
    )
    half = HEAD_DIM // 2
    scale = math.log2(math.e) / math.sqrt(HEAD_DIM)
    for count in groups:
        group, tiles = tiles[:count], tiles[count:]
        rows = jnp.concatenate([t[...] for t in group], axis=0).astype(F32)
        rows = norm(rows, gain_ref[...]).astype(BF)
        span = slice(at, at + rows.shape[0])
        at += rows.shape[0]
        mapped = lax.dot_general(
            weight, rows, (((1,), (1,)), ((), ())), preferred_element_type=F32
        )
        cos, sin = cos_ref[:, span], sin_ref[:, span]

        def turn(u):
            first, second = u[:half], u[half:]
            return jnp.concatenate([first * cos - second * sin, second * cos + first * sin], axis=0)

        part = [mapped[k * HEAD_DIM : (k + 1) * HEAD_DIM] for k in range(6)]
        q_out[:, span] = (turn(part[0]) * scale).astype(BF)
        kv_out[:HEAD_DIM, span] = turn(part[1]).astype(BF)
        kv_out[HEAD_DIM:, span] = part[2].astype(BF)
        other_out[:HEAD_DIM, span] = (turn(part[3]) * scale).astype(BF)
        other_out[HEAD_DIM : 2 * HEAD_DIM, span] = turn(part[4]).astype(BF)
        other_out[2 * HEAD_DIM :, span] = part[5].astype(BF)


def split_rows(m):
    hi = m.astype(BF)
    rest = m - hi.astype(F32)
    mid = rest.astype(BF)
    low = (rest - mid.astype(F32)).astype(BF)
    pad = jnp.zeros((13, m.shape[1]), BF)
    return jnp.concatenate([-hi, -mid, -low, pad], axis=0)


def attend_chunks(chunks, q_ref, m_ref, o_ref, k_all, v_all, flag):
    keys = k_all.shape[0]
    queries = q_ref.shape[1]
    step = keys if keys <= 2048 else max(d for d in (2048, 1536, 1024) if keys % d == 0)
    turns = queries // (2 * QUERY_BLOCK)
    at = 0
    for ref in chunks:
        n = ref.shape[1]
        ones = jnp.ones((16, n), BF)
        k_all[at : at + n, :] = jnp.concatenate([ref[-2 * HEAD_DIM : -HEAD_DIM, :], ones], axis=0).T
        v_all[:, at : at + n] = jnp.concatenate([ref[-HEAD_DIM:, :], ones], axis=0)
        at += n
    flag[0] = 1

    def attempt(tries, carry):
        @pl.when(flag[0] == 1)
        def _():
            o_ref[...] = jnp.zeros_like(o_ref)

            def block(t, carry):
                rows = pl.ds(pl.multiple_of((t // turns) * step, step), step)
                for i in range(2):
                    col = (t % turns) * (2 * QUERY_BLOCK) + i * QUERY_BLOCK
                    cols = pl.ds(pl.multiple_of(col, QUERY_BLOCK), QUERY_BLOCK)
                    s = jnp.dot(k_all[rows, :], q_ref[:, cols], preferred_element_type=F32)
                    p = jnp.exp2(s).astype(BF)
                    o_ref[:, cols] += jnp.dot(v_all[:, rows], p, preferred_element_type=F32)
                return carry

            lax.fori_loop(0, keys // step * turns, block, 0)
            mass = o_ref[HEAD_DIM : HEAD_DIM + 8, :]
            bad = jnp.max(jnp.where(mass < LIMIT, 0.0, 1.0)) > 0.0
            flag[0] = jnp.where(jnp.logical_and(bad, tries == 0), 1, 0)

            @pl.when(flag[0] == 1)
            def _():
                m_ref[1:2, :] = jnp.zeros((1, queries), F32)

                def top_block(t, carry):
                    rows = pl.ds(pl.multiple_of((t // 8) * 512, 512), 512)
                    cols = pl.ds(pl.multiple_of((t % 8) * 256, 256), 256)
                    s = jnp.dot(k_all[rows, :], q_ref[:, cols], preferred_element_type=F32)
                    m_ref[1:2, cols] = jnp.maximum(
                        m_ref[1:2, cols], jnp.max(s, axis=0, keepdims=True)
                    )
                    return carry

                lax.fori_loop(0, keys // 512 * (queries // 256), top_block, 0)
                fresh = m_ref[0:1, :] + m_ref[1:2, :]
                m_ref[0:1, :] = fresh
                q_ref[HEAD_DIM:, :] = split_rows(fresh)

        return carry

    lax.fori_loop(0, 2, attempt, 0)


def first_kernel(own_q, swapped, kv_ref, q_out, start_out, m_ref, o_ref, q_ref, k_all, v_all, flag):
    n = own_q.shape[1]
    q_ref[:HEAD_DIM, :n] = own_q[...]
    q_ref[:HEAD_DIM, n:] = swapped[:HEAD_DIM, :]
    some = kv_ref[:HEAD_DIM, :512].T

    def start(i, carry):
        cols = pl.ds(pl.multiple_of(i * QUERY_BLOCK, QUERY_BLOCK), QUERY_BLOCK)
        s = jnp.dot(some, q_ref[:HEAD_DIM, cols], preferred_element_type=F32)
        m_ref[:, cols] = jnp.broadcast_to(jnp.max(s, axis=0, keepdims=True), (8, QUERY_BLOCK))
        return carry

    lax.fori_loop(0, 2 * n // QUERY_BLOCK, start, 0)
    q_ref[HEAD_DIM:, :] = split_rows(m_ref[0:1, :])
    q_out[...] = q_ref[...]
    start_out[...] = m_ref[...]
    attend_chunks([kv_ref], q_ref, m_ref, o_ref, k_all, v_all, flag)


def next_kernel(count, *refs):
    chunks, rest = refs[:count], refs[count:]
    q_in, m_in, m_ref, o_ref, q_ref, k_all, v_all, flag = rest
    q_ref[...] = q_in[...]
    m_ref[...] = m_in[...]
    attend_chunks(chunks, q_ref, m_ref, o_ref, k_all, v_all, flag)


def last_kernel(count, done, place, *refs):
    chunks, rest = refs[:count], refs[count:]
    q_in, m_in = rest[:2]
    tops, sums = rest[2 : 2 + done], rest[2 + done : 2 + 2 * done]
    own_ref, swap_ref, q_ref, m_ref, o_ref, k_all, v_all, flag = rest[2 + 2 * done :]
    q_ref[...] = q_in[...]
    m_ref[...] = m_in[...]
    attend_chunks(chunks, q_ref, m_ref, o_ref, k_all, v_all, flag)
    top = m_ref[0:1, :]
    for t in tops:
        top = jnp.maximum(top, t[0:1, :])
    total = o_ref[...] * jnp.exp2(m_ref[0:1, :] - top)
    for t, o in zip(tops, sums):
        total = total + o[...] * jnp.exp2(t[0:1, :] - top)
    half = total.shape[1] // 2
    for out_ref, lower in ((own_ref, 0), (swap_ref, half)):
        for s in range(half // 128):
            cols = slice(lower + s * 128, lower + (s + 1) * 128)
            mass = total[HEAD_DIM : HEAD_DIM + 1, cols]
            target = pl.ds(pl.multiple_of(place[s] * 128, 128), 128)
            out_ref[:, target] = (total[:HEAD_DIM, cols] / mass).astype(BF)


def add_heads(slots, pieces, col_ref, c, weight_ref, base_ref, out_ref):
    rows = []
    for slot in slots:
        for head in (c, 1 - c):
            spot = pl.multiple_of(col_ref[slot] * 160 + head * 80, 16)
            rows.append(weight_ref[pl.ds(spot, 80), :])
    weight = jnp.concatenate(rows, axis=0)

    def block(i, carry):
        spot = pl.ds(pl.multiple_of(i * 512, 512), 512)
        lhs = jnp.concatenate([p[:, spot] for p in pieces], axis=0).T
        out_ref[spot, :] = base_ref[spot, :] + jnp.dot(lhs, weight, preferred_element_type=F32)
        return carry

    lax.fori_loop(0, out_ref.shape[0] // 512, block, 0)


def mix_first_kernel(col_ref, place_ref, weight_ref, *refs):
    pieces, tiles, out_ref = refs[:4], refs[4:13], refs[13]
    for slot in range(8):
        row = col_ref[slot] * 128
        if slot < 7:
            spot = pl.ds(pl.multiple_of(row, 128), 128)
            out_ref[spot, :] = tiles[slot][...].astype(F32)
        else:
            for k in range(2):
                spot = pl.ds(pl.multiple_of(row + k * 64, 64), 64)
                out_ref[spot, :] = tiles[7 + k][...].astype(F32)
    add_heads((0, 1, 2, 3), pieces, col_ref, place_ref[0], weight_ref, out_ref, out_ref)


def mix_next_kernel(col_ref, place_ref, weight_ref, *refs):
    pieces, base_ref, out_ref = refs[:3], refs[3], refs[4]
    add_heads((4, 5, 6), pieces, col_ref, place_ref[0], weight_ref, base_ref, out_ref)


def merge_kernel(col_ref, place_ref, out_weight, *refs):
    pieces, rest = refs[:2], refs[2:]
    base_ref, gain_ref, up_weight, bias_ref, hidden_a, hidden_b, mixed_all, merged = rest
    c, x, zh = place_ref[0], place_ref[1], place_ref[2]
    width = out_weight.shape[1]
    add_heads((7,), pieces, col_ref, c, out_weight, base_ref, mixed_all)
    r = lax.broadcasted_iota(jnp.int32, (128, 128), 0)
    t = lax.broadcasted_iota(jnp.int32, (128, 128), 1)
    a, b, u, w = r >> 6, (r >> 5) & 1, (r >> 3) & 3, r & 7
    pick = ((2 * u + a) * 16 + 2 * w + b == t).astype(BF)

    def settle(turn, carry):
        for k in range(4):
            s = turn * 4 + k
            spot = pl.ds(pl.multiple_of(col_ref[s] * 128, 128), 128)
            normed = norm(mixed_all[spot, :], gain_ref[...]).astype(BF)
            ordered = jnp.dot(pick, normed, preferred_element_type=F32).astype(BF)
            rows = pl.ds(pl.multiple_of(s * 32, 32), 32)
            for q in range(4):
                merged[q, rows, :] = ordered[q * 32 : (q + 1) * 32]
        return carry

    lax.fori_loop(0, 2, settle, 0)
    z = bias_ref[...]
    for q in range(4):
        z = z + jnp.dot(
            merged[q], up_weight[q * width : (q + 1) * width, :], preferred_element_type=F32
        )
    hidden = (0.5 * z * (1.0 + lax.erf(z * (1.0 / math.sqrt(2.0))))).astype(BF)
    n = hidden.shape[0]
    rows = lax.broadcasted_iota(jnp.int32, (n, n), 0)
    lane = lax.broadcasted_iota(jnp.int32, (1, n), 1)
    col = jnp.zeros((1, n), jnp.int32)
    for s in range(8):
        col = jnp.where((lane >> 5) == s, col_ref[s], col)
    raster = ((lane >> 3) & 3) * 64 + col * 8 + (lane & 7)
    owner = raster >> 5
    ahead = ((owner >> 1) - x) & 3
    other_half = (owner & 1) ^ zh
    place_a = ahead * 64 + other_half * 32 + (raster & 31)
    place_b = other_half * 128 + ahead * 32 + (raster & 31)
    for place, out in ((place_a, hidden_a), (place_b, hidden_b)):
        out[...] = jnp.dot(
            (rows == place).astype(BF), hidden, preferred_element_type=F32
        ).astype(BF)


def spread(own, axis, across, dim, extras=()):
    forward, backward = shift(axis, 1), shift(axis, -1)
    half = own.shape[dim] // 2
    plus, minus, mirror = send(own, forward), send(own, backward), send(own, across)
    plus, minus, mirror, extras = lax.optimization_barrier((plus, minus, mirror, extras))
    two = send(plus, forward)
    mirror_plus = send(plus, across)
    mirror_minus = send(mirror, backward)
    far_low = send(lax.slice_in_dim(mirror_plus, 0, half, axis=dim), forward)
    far_high = send(lax.slice_in_dim(two, half, 2 * half, axis=dim), across)
    return [own, plus, minus, mirror, two, mirror_plus, mirror_minus, far_low, far_high], extras


def shards(
    patches,
    norm_gain,
    query_weight,
    key_weight,
    value_weight,
    out_weight,
    merge_gain,
    up_weight,
    up_bias,
    down_weight,
    down_bias,
):
    band_height, tile_width, model_width = patches.shape
    tile = band_height * tile_width
    band = tile * 8
    y, zl, c = lax.axis_index("y"), lax.axis_index("zl"), lax.axis_index("c")
    x, zh = lax.axis_index("x"), lax.axis_index("zh")
    row_index = (y * 2 + zl) * 2 + c
    sds = jax.ShapeDtypeStruct

    slot_x = jnp.stack([x, x - 1, x + 1, x, x + 2, x - 1, x + 1, x + 2]) % 4
    slot_z = jnp.stack([zh, zh, zh, 1 - zh, zh, 1 - zh, 1 - zh, 1 - zh])
    slot_col = (slot_x * 2 + slot_z).astype(jnp.int32)
    local = np.arange(tile)
    row_coord = (row_index * band_height + jnp.tile(local // tile_width, 8)).astype(F32)
    col_coord = (
        (slot_col[:, None] * tile_width + (local % tile_width)[None, :]).astype(F32).reshape(-1)
    )
    frequency = 1.0 / 10000.0 ** (
        jnp.arange(HEAD_DIM // 4, dtype=F32) * 2.0 / (HEAD_DIM // 2)
    )
    angles = jnp.concatenate(
        [frequency[:, None] * row_coord[None, :], frequency[:, None] * col_coord[None, :]], axis=0
    )
    cos, sin = jnp.cos(angles), jnp.sin(angles)

    mirror_x = pairs(lambda d: {"zh": 1 - d["zh"]})
    tokens = patches.reshape(tile, model_width)
    gains = [v.reshape(1, -1) for v in (norm_gain, merge_gain, up_bias)]
    tiles, (cos, sin, gains) = spread(tokens, "x", mirror_x, 0, (cos, sin, gains))
    shapes = (
        sds((HEAD_DIM, band), BF),
        sds((2 * HEAD_DIM, band), BF),
        sds((3 * HEAD_DIM, band), BF),
    )
    fixed = [("s", c.reshape(1).astype(jnp.int32)), ("v", gains[0])]
    fixed += [("v", w.T) for w in (query_weight, key_weight, value_weight)]
    fixed += [("v", cos), ("v", sin)]
    mapped = ()
    for k, (groups, used) in enumerate(
        (((2, 2), tiles[:4]), ((2, 1), tiles[4:7]), ((2,), tiles[7:]))
    ):
        first = (0, 4, 7)[k]
        spot = len(fixed) + len(used)
        mapped = call(
            functools.partial(project_kernel, groups, first * tile),
            shapes,
            fixed + [("v", t) for t in used] + [("v", t) for t in mapped],
            flops=2 * tile * (4, 3, 1)[k] * model_width * 480,
            alias={spot + o: o for o in range(len(mapped))},
        )
    q_own, kv_own, other = mapped
    n = 2 * band
    swap = pairs(lambda d: {"c": 1 - d["c"]})
    mirror_y = pairs(lambda d: {"zl": 1 - d["zl"]})
    swapped = send(other, swap)
    kv = jnp.concatenate([kv_own, swapped[HEAD_DIM:]], axis=1)
    chunks, _ = spread(kv, "y", mirror_y, 1)
    groups = (chunks[1:4], chunks[4:7], chunks[7:])
    q_shape, m_shape, o_shape = sds((96, n), BF), sds((8, n), F32), sds((96, n), F32)

    def scratch(keys):
        return [
            pltpu.VMEM((96, n), BF),
            pltpu.VMEM((keys, 96), BF),
            pltpu.VMEM((96, keys), BF),
            pltpu.SMEM((1,), jnp.int32),
        ]

    work = lambda keys: dict(flops=2 * n * keys * 512, exps=n * keys, nbytes=4 * n * 96)
    q, start, top, part = call(
        first_kernel,
        (q_shape, m_shape, m_shape, o_shape),
        [("v", q_own), ("v", swapped), ("v", kv)],
        scratch(n),
        **work(n),
    )
    tops, parts = [top], [part]
    for chunks in groups[:-1]:
        keys = sum(t.shape[1] for t in chunks)
        top, part = call(
            functools.partial(next_kernel, len(chunks)),
            (m_shape, o_shape),
            [("v", t) for t in chunks] + [("v", q), ("v", start)],
            scratch(keys),
            **work(keys),
        )
        tops.append(top)
        parts.append(part)
    final = scratch(n)
    half_shape = sds((HEAD_DIM, band), BF)
    attended, partner = call(
        functools.partial(last_kernel, 2, len(tops)),
        (half_shape, half_shape),
        [("s", slot_col)] + [("v", t) for t in (*groups[-1], q, start, *tops, *parts)],
        [final[0], pltpu.VMEM((8, n), F32), pltpu.VMEM((96, n), F32), *final[1:]],
        **work(n),
    )
    attended = jnp.concatenate([attended, send(partner, swap)], axis=0)
    pieces, _ = spread(attended, "x", mirror_x, 0)
    where = [
        ("s", slot_col),
        ("s", jnp.stack([c, x, zh]).astype(jnp.int32)),
        ("v", out_weight),
    ]
    total = sds((band, model_width), F32)
    total_flops = 2 * band * model_width * model_width
    mixed = call(
        mix_first_kernel,
        total,
        where + [("v", t) for t in (*pieces[:4], *tiles)],
        flops=total_flops // 2,
        grant=10,
    )
    mixed = call(
        mix_next_kernel,
        total,
        where + [("v", t) for t in (*pieces[4:7], mixed)],
        flops=3 * total_flops // 8,
        grant=10,
        alias={6: 0},
    )
    hidden_a, hidden_b = call(
        merge_kernel,
        (sds((256, up_weight.shape[1]), BF),) * 2,
        where
        + [("v", t) for t in (*pieces[7:], mixed, gains[1])]
        + [("v", up_weight), ("v", gains[2])],
        [pltpu.VMEM((band, model_width), F32), pltpu.VMEM((4, 256, model_width), BF)],
        flops=2 * 256 * 5120 * 640 + total_flops // 8,
        grant=18,
    )
    return scatter_output(hidden_a, hidden_b, down_weight, down_bias, mirror_x)


def ring(block, rows):
    forward, backward = shift("x", 1), shift("x", -1)
    half = block.shape[1] // 2
    part = lambda k: block[k * rows : (k + 1) * rows]
    ahead, behind, far = part(1), part(3), part(2)
    from_behind = send(far[:, :half], forward)
    from_ahead = send(far[:, half:], backward)
    add = lambda p, q: (p.astype(F32) + q.astype(F32)).astype(BF)
    onward = jnp.concatenate([add(ahead[:, :half], from_behind), ahead[:, half:]], axis=1)
    back = jnp.concatenate([behind[:, :half], add(behind[:, half:], from_ahead)], axis=1)
    got_behind, got_ahead = send(onward, forward), send(back, backward)
    return part(0).astype(F32) + got_behind.astype(F32) + got_ahead.astype(F32)


def scatter_output(hidden_a, hidden_b, down_weight, down_bias, mirror):
    split = 4608
    part_b = jnp.dot(
        hidden_b, down_weight[:, split:], preferred_element_type=F32
    ).astype(BF)
    give_b, hidden_a = lax.optimization_barrier((part_b[128:], hidden_a))
    got_b = send(give_b, mirror)
    part_a = jnp.dot(
        hidden_a, down_weight[:, :split], preferred_element_type=F32
    ).astype(BF)
    total_a = ring(part_a, 64)
    got_a = send(total_a[32:].astype(BF), mirror)
    block_b = (part_b[:128].astype(F32) + got_b.astype(F32)).astype(BF)
    total_b = ring(block_b, 32)
    total_a = total_a[:32] + got_a.astype(F32)
    return (jnp.concatenate([total_a, total_b], axis=1) + down_bias[None, :]).astype(BF)


def solution(mesh):
    fine = Mesh(mesh.devices.reshape(SIZES), AXES)
    row, col = ("y", "zl", "c"), ("x", "zh")
    placed = (
        P(row, col, None),
        P(),
        P(None, col),
        P(None, col),
        P(None, col),
        P(),
        P(),
        P(None, col),
        P(col),
        P(col, None),
        P(),
    )

    return jax.shard_map(
        shards, mesh=fine, in_specs=placed, out_specs=P(row + col, None), check_vma=False
    )
```

```python
import functools
import math

import jax
import jax.numpy as jnp
import numpy as np
from jax import lax
from jax.experimental import pallas as pl
from jax.experimental.pallas import tpu as pltpu
from jax.sharding import Mesh
from jax.sharding import PartitionSpec as P


HEAD_DIM = 80
EPSILON = 1e-06
AXES = ("y", "zl", "c", "x", "zh")
SIZES = (4, 2, 2, 4, 2)
BF = jnp.bfloat16
F32 = jnp.float32
QUERY_BLOCK = 512
LIMIT = 2.0**64


def pairs(move):
    result = []
    for place in np.ndindex(*SIZES):
        there = dict(zip(AXES, place))
        there.update(move(there))
        target = tuple(there[a] % n for a, n in zip(AXES, SIZES))
        result.append(
            (int(np.ravel_multi_index(place, SIZES)), int(np.ravel_multi_index(target, SIZES)))
        )
    return result


def shift(axis, step):
    return pairs(lambda d: {axis: d[axis] + step})


def send(value, perm):
    return lax.ppermute(value, AXES, perm)


def vmem():
    return pl.BlockSpec(memory_space=pltpu.VMEM)


def smem():
    return pl.BlockSpec(memory_space=pltpu.SMEM)


def call(kernel, outs, ins, scratch=(), flops=0, nbytes=0, exps=0, grant=8, alias=None):
    specs = [smem() if k == "s" else vmem() for k, _ in ins]
    return pl.pallas_call(
        kernel,
        out_shape=outs,
        in_specs=specs,
        out_specs=jax.tree.map(lambda _: vmem(), outs),
        scratch_shapes=list(scratch),
        input_output_aliases=alias or {},
        cost_estimate=pl.CostEstimate(flops=flops, bytes_accessed=nbytes, transcendentals=exps),
        compiler_params=pltpu.CompilerParams(vmem_limit_bytes=grant * 2**20),
    )(*[a for _, a in ins])


def norm(values, gain):
    center = values - jnp.mean(values, axis=-1, keepdims=True)
    spread = jnp.mean(center * center, axis=-1, keepdims=True)
    return center * lax.rsqrt(spread + EPSILON) * gain


def project_kernel(groups, at, c_ref, gain_ref, wq, wk, wv, cos_ref, sin_ref, *refs):
    tiles = refs[: sum(groups)]
    q_out, kv_out, other_out = refs[-3:]
    mine = pl.multiple_of(c_ref[0] * HEAD_DIM, 16)
    others = pl.multiple_of((1 - c_ref[0]) * HEAD_DIM, 16)
    weight = jnp.concatenate(
        [w[pl.ds(o, HEAD_DIM), :] for o in (mine, others) for w in (wq, wk, wv)], axis=0
    )
    half = HEAD_DIM // 2
    scale = math.log2(math.e) / math.sqrt(HEAD_DIM)
    for count in groups:
        group, tiles = tiles[:count], tiles[count:]
        rows = jnp.concatenate([t[...] for t in group], axis=0).astype(F32)
        rows = norm(rows, gain_ref[...]).astype(BF)
        span = slice(at, at + rows.shape[0])
        at += rows.shape[0]
        mapped = lax.dot_general(
            weight, rows, (((1,), (1,)), ((), ())), preferred_element_type=F32
        )
        cos, sin = cos_ref[:, span], sin_ref[:, span]

        def turn(u):
            first, second = u[:half], u[half:]
            return jnp.concatenate([first * cos - second * sin, second * cos + first * sin], axis=0)

        part = [mapped[k * HEAD_DIM : (k + 1) * HEAD_DIM] for k in range(6)]
        q_out[:, span] = (turn(part[0]) * scale).astype(BF)
        kv_out[:HEAD_DIM, span] = turn(part[1]).astype(BF)
        kv_out[HEAD_DIM:, span] = part[2].astype(BF)
        other_out[:HEAD_DIM, span] = (turn(part[3]) * scale).astype(BF)
        other_out[HEAD_DIM : 2 * HEAD_DIM, span] = turn(part[4]).astype(BF)
        other_out[2 * HEAD_DIM :, span] = part[5].astype(BF)


def split_rows(m):
    hi = m.astype(BF)
    rest = m - hi.astype(F32)
    mid = rest.astype(BF)
    low = (rest - mid.astype(F32)).astype(BF)
    pad = jnp.zeros((13, m.shape[1]), BF)
    return jnp.concatenate([-hi, -mid, -low, pad], axis=0)


def attend_chunks(chunks, q_ref, m_ref, o_ref, k_all, v_all, flag):
    keys = k_all.shape[0]
    queries = q_ref.shape[1]
    step = keys if keys <= 2048 else max(d for d in (1536, 1024) if keys % d == 0)
    turns = queries // (2 * QUERY_BLOCK)
    at = 0
    for ref in chunks:
        n = ref.shape[1]
        ones = jnp.ones((16, n), BF)
        k_all[at : at + n, :] = jnp.concatenate([ref[-2 * HEAD_DIM : -HEAD_DIM, :], ones], axis=0).T
        v_all[:, at : at + n] = jnp.concatenate([ref[-HEAD_DIM:, :], ones], axis=0)
        at += n
    flag[0] = 1

    def attempt(tries, carry):
        @pl.when(flag[0] == 1)
        def _():
            o_ref[...] = jnp.zeros_like(o_ref)

            def block(t, carry):
                rows = pl.ds(pl.multiple_of((t // turns) * step, step), step)
                for i in range(2):
                    col = (t % turns) * (2 * QUERY_BLOCK) + i * QUERY_BLOCK
                    cols = pl.ds(pl.multiple_of(col, QUERY_BLOCK), QUERY_BLOCK)
                    s = jnp.dot(k_all[rows, :], q_ref[:, cols], preferred_element_type=F32)
                    p = jnp.exp2(s).astype(BF)
                    o_ref[:, cols] += jnp.dot(v_all[:, rows], p, preferred_element_type=F32)
                return carry

            lax.fori_loop(0, keys // step * turns, block, 0)
            mass = o_ref[HEAD_DIM : HEAD_DIM + 8, :]
            bad = jnp.max(jnp.where(mass < LIMIT, 0.0, 1.0)) > 0.0
            flag[0] = jnp.where(jnp.logical_and(bad, tries == 0), 1, 0)

            @pl.when(flag[0] == 1)
            def _():
                m_ref[1:2, :] = jnp.zeros((1, queries), F32)

                def top_block(t, carry):
                    rows = pl.ds(pl.multiple_of((t // 8) * 512, 512), 512)
                    cols = pl.ds(pl.multiple_of((t % 8) * 256, 256), 256)
                    s = jnp.dot(k_all[rows, :], q_ref[:, cols], preferred_element_type=F32)
                    m_ref[1:2, cols] = jnp.maximum(
                        m_ref[1:2, cols], jnp.max(s, axis=0, keepdims=True)
                    )
                    return carry

                lax.fori_loop(0, keys // 512 * (queries // 256), top_block, 0)
                fresh = m_ref[0:1, :] + m_ref[1:2, :]
                m_ref[0:1, :] = fresh
                q_ref[HEAD_DIM:, :] = split_rows(fresh)

        return carry

    lax.fori_loop(0, 2, attempt, 0)


def first_kernel(own_q, swapped, kv_ref, q_out, start_out, m_ref, o_ref, q_ref, k_all, v_all, flag):
    n = own_q.shape[1]
    q_ref[:HEAD_DIM, :n] = own_q[...]
    q_ref[:HEAD_DIM, n:] = swapped[:HEAD_DIM, :]
    some = kv_ref[:HEAD_DIM, :512].T

    def start(i, carry):
        cols = pl.ds(pl.multiple_of(i * QUERY_BLOCK, QUERY_BLOCK), QUERY_BLOCK)
        s = jnp.dot(some, q_ref[:HEAD_DIM, cols], preferred_element_type=F32)
        m_ref[:, cols] = jnp.broadcast_to(jnp.max(s, axis=0, keepdims=True), (8, QUERY_BLOCK))
        return carry

    lax.fori_loop(0, 2 * n // QUERY_BLOCK, start, 0)
    q_ref[HEAD_DIM:, :] = split_rows(m_ref[0:1, :])
    q_out[...] = q_ref[...]
    start_out[...] = m_ref[...]
    attend_chunks([kv_ref, swapped], q_ref, m_ref, o_ref, k_all, v_all, flag)


def next_kernel(count, *refs):
    chunks, rest = refs[:count], refs[count:]
    q_in, m_in, m_ref, o_ref, q_ref, k_all, v_all, flag = rest
    q_ref[...] = q_in[...]
    m_ref[...] = m_in[...]
    attend_chunks(chunks, q_ref, m_ref, o_ref, k_all, v_all, flag)


def last_kernel(count, done, place, *refs):
    chunks, rest = refs[:count], refs[count:]
    q_in, m_in = rest[:2]
    tops, sums = rest[2 : 2 + done], rest[2 + done : 2 + 2 * done]
    own_ref, swap_ref, q_ref, m_ref, o_ref, k_all, v_all, flag = rest[2 + 2 * done :]
    q_ref[...] = q_in[...]
    m_ref[...] = m_in[...]
    attend_chunks(chunks, q_ref, m_ref, o_ref, k_all, v_all, flag)
    half = o_ref.shape[1] // 2
    for out_ref, lower in ((own_ref, 0), (swap_ref, half)):

        def block(turn, carry, out_ref=out_ref, lower=lower):
            for k in range(4):
                slot = turn * 4 + k
                cols = pl.ds(pl.multiple_of(lower + slot * 128, 128), 128)
                own_top = m_ref[0:1, cols]
                top = own_top
                for t in tops:
                    top = jnp.maximum(top, t[0:1, cols])
                total = o_ref[:, cols] * jnp.exp2(own_top - top)
                for t, o in zip(tops, sums):
                    total = total + o[:, cols] * jnp.exp2(t[0:1, cols] - top)
                target = pl.ds(pl.multiple_of(place[slot] * 128, 128), 128)
                mass = total[HEAD_DIM : HEAD_DIM + 1]
                out_ref[:, target] = (total[:HEAD_DIM] / mass).astype(BF)
            return carry

        lax.fori_loop(0, half // 512, block, 0)


def add_heads(slots, pieces, col_ref, c, weight_ref, base_ref, out_ref):
    rows = []
    for slot in slots:
        for head in (c, 1 - c):
            spot = pl.multiple_of(col_ref[slot] * 160 + head * 80, 16)
            rows.append(weight_ref[pl.ds(spot, 80), :])
    weight = jnp.concatenate(rows, axis=0)

    def block(i, carry):
        spot = pl.ds(pl.multiple_of(i * 512, 512), 512)
        lhs = jnp.concatenate([p[:, spot] for p in pieces], axis=0).T
        out_ref[spot, :] = base_ref[spot, :] + jnp.dot(lhs, weight, preferred_element_type=F32)
        return carry

    lax.fori_loop(0, out_ref.shape[0] // 512, block, 0)


def mix_first_kernel(col_ref, place_ref, weight_ref, *refs):
    pieces, tiles, out_ref = refs[:4], refs[4:13], refs[13]
    starts = [col_ref[slot] * 128 for slot in range(8)] + [col_ref[7] * 128 + 64]
    for tile, start in zip(tiles, starts):

        def copy(i, carry, tile=tile, start=start):
            rows = pl.ds(pl.multiple_of(i * 32, 32), 32)
            spot = pl.ds(pl.multiple_of(start + i * 32, 32), 32)
            out_ref[spot, :] = tile[rows, :].astype(F32)
            return carry

        lax.fori_loop(0, tile.shape[0] // 32, copy, 0)
    add_heads((0, 1, 2, 3), pieces, col_ref, place_ref[0], weight_ref, out_ref, out_ref)


def mix_next_kernel(col_ref, place_ref, weight_ref, *refs):
    pieces, base_ref, out_ref = refs[:3], refs[3], refs[4]
    add_heads((4, 5, 6), pieces, col_ref, place_ref[0], weight_ref, base_ref, out_ref)


def merge_kernel(col_ref, place_ref, out_weight, *refs):
    pieces, rest = refs[:2], refs[2:]
    base_ref, gain_ref, up_weight, bias_ref, hidden_a, hidden_b, mixed_all, merged = rest
    c, x, zh = place_ref[0], place_ref[1], place_ref[2]
    width = out_weight.shape[1]
    add_heads((7,), pieces, col_ref, c, out_weight, base_ref, mixed_all)
    r = lax.broadcasted_iota(jnp.int32, (128, 128), 0)
    t = lax.broadcasted_iota(jnp.int32, (128, 128), 1)
    a, b, u, w = r >> 6, (r >> 5) & 1, (r >> 3) & 3, r & 7
    pick = ((2 * u + a) * 16 + 2 * w + b == t).astype(BF)

    def settle(turn, carry):
        for k in range(4):
            s = turn * 4 + k
            spot = pl.ds(pl.multiple_of(col_ref[s] * 128, 128), 128)
            normed = norm(mixed_all[spot, :], gain_ref[...]).astype(BF)
            ordered = jnp.dot(pick, normed, preferred_element_type=F32).astype(BF)
            rows = pl.ds(pl.multiple_of(s * 32, 32), 32)
            for q in range(4):
                merged[q, rows, :] = ordered[q * 32 : (q + 1) * 32]
        return carry

    lax.fori_loop(0, 2, settle, 0)
    z = bias_ref[...]
    for q in range(4):
        z = z + jnp.dot(
            merged[q], up_weight[q * width : (q + 1) * width, :], preferred_element_type=F32
        )
    hidden = (0.5 * z * (1.0 + lax.erf(z * (1.0 / math.sqrt(2.0))))).astype(BF)
    n = hidden.shape[0]
    rows = lax.broadcasted_iota(jnp.int32, (n, n), 0)
    lane = lax.broadcasted_iota(jnp.int32, (1, n), 1)
    col = jnp.zeros((1, n), jnp.int32)
    for s in range(8):
        col = jnp.where((lane >> 5) == s, col_ref[s], col)
    raster = ((lane >> 3) & 3) * 64 + col * 8 + (lane & 7)
    owner = raster >> 5
    ahead = ((owner >> 1) - x) & 3
    other_half = (owner & 1) ^ zh
    place_a = ahead * 64 + other_half * 32 + (raster & 31)
    place_b = other_half * 128 + ahead * 32 + (raster & 31)
    for place, out in ((place_a, hidden_a), (place_b, hidden_b)):
        out[...] = jnp.dot(
            (rows == place).astype(BF), hidden, preferred_element_type=F32
        ).astype(BF)


def spread(own, axis, across, dim, extras=()):
    forward, backward = shift(axis, 1), shift(axis, -1)
    half = own.shape[dim] // 2
    plus, minus, mirror = send(own, forward), send(own, backward), send(own, across)
    plus, minus, mirror, extras = lax.optimization_barrier((plus, minus, mirror, extras))
    two = send(plus, forward)
    mirror_plus = send(plus, across)
    mirror_minus = send(mirror, backward)
    far_low = send(lax.slice_in_dim(mirror_plus, 0, half, axis=dim), forward)
    far_high = send(lax.slice_in_dim(two, half, 2 * half, axis=dim), across)
    return [own, plus, minus, mirror, two, mirror_plus, mirror_minus, far_low, far_high], extras


def shards(
    patches,
    norm_gain,
    query_weight,
    key_weight,
    value_weight,
    out_weight,
    merge_gain,
    up_weight,
    up_bias,
    down_weight,
    down_bias,
):
    band_height, tile_width, model_width = patches.shape
    tile = band_height * tile_width
    band = tile * 8
    y, zl, c = lax.axis_index("y"), lax.axis_index("zl"), lax.axis_index("c")
    x, zh = lax.axis_index("x"), lax.axis_index("zh")
    row_index = (y * 2 + zl) * 2 + c
    sds = jax.ShapeDtypeStruct

    slot_x = jnp.stack([x, x - 1, x + 1, x, x + 2, x - 1, x + 1, x + 2]) % 4
    slot_z = jnp.stack([zh, zh, zh, 1 - zh, zh, 1 - zh, 1 - zh, 1 - zh])
    slot_col = (slot_x * 2 + slot_z).astype(jnp.int32)
    local = np.arange(tile)
    row_coord = (row_index * band_height + jnp.tile(local // tile_width, 8)).astype(F32)
    col_coord = (
        (slot_col[:, None] * tile_width + (local % tile_width)[None, :]).astype(F32).reshape(-1)
    )
    frequency = 1.0 / 10000.0 ** (
        jnp.arange(HEAD_DIM // 4, dtype=F32) * 2.0 / (HEAD_DIM // 2)
    )
    angles = jnp.concatenate(
        [frequency[:, None] * row_coord[None, :], frequency[:, None] * col_coord[None, :]], axis=0
    )
    cos, sin = jnp.cos(angles), jnp.sin(angles)

    mirror_x = pairs(lambda d: {"zh": 1 - d["zh"]})
    tokens = patches.reshape(tile, model_width)
    gains = [v.reshape(1, -1) for v in (norm_gain, merge_gain, up_bias)]
    tiles, (cos, sin, gains) = spread(tokens, "x", mirror_x, 0, (cos, sin, gains))
    shapes = (
        sds((HEAD_DIM, band), BF),
        sds((2 * HEAD_DIM, band), BF),
        sds((3 * HEAD_DIM, band), BF),
    )
    fixed = [("s", c.reshape(1).astype(jnp.int32)), ("v", gains[0])]
    fixed += [("v", w.T) for w in (query_weight, key_weight, value_weight)]
    fixed += [("v", cos), ("v", sin)]
    mapped = ()
    for k, (groups, used) in enumerate(
        (((2, 2), tiles[:4]), ((2, 1), tiles[4:7]), ((2,), tiles[7:]))
    ):
        first = (0, 4, 7)[k]
        spot = len(fixed) + len(used)
        mapped = call(
            functools.partial(project_kernel, groups, first * tile),
            shapes,
            fixed + [("v", t) for t in used] + [("v", t) for t in mapped],
            flops=2 * tile * (4, 3, 1)[k] * model_width * 480,
            alias={spot + o: o for o in range(len(mapped))},
        )
    q_own, kv_own, other = mapped
    n = 2 * band
    swap = pairs(lambda d: {"c": 1 - d["c"]})
    mirror_y = pairs(lambda d: {"zl": 1 - d["zl"]})
    swapped = send(other, swap)
    forward, backward = shift("y", 1), shift("y", -1)
    near = [send(kv_own, p) for p in (forward, backward, mirror_y)]
    near += [send(swapped[HEAD_DIM:], p) for p in (forward, backward, mirror_y)]
    near = lax.optimization_barrier(near)
    plus = jnp.concatenate([near[0], near[3]], axis=1)
    mirror = jnp.concatenate([near[2], near[5]], axis=1)
    two, mirror_plus = send(plus, forward), send(plus, mirror_y)
    mirror_minus = send(mirror, backward)
    far = [send(mirror_plus[:, :band], forward), send(two[:, band:], mirror_y)]
    groups = (near, [two, mirror_plus, mirror_minus], far)
    q_shape, m_shape, o_shape = sds((96, n), BF), sds((8, n), F32), sds((96, n), F32)

    def scratch(keys):
        return [
            pltpu.VMEM((96, n), BF),
            pltpu.VMEM((keys, 96), BF),
            pltpu.VMEM((96, keys), BF),
            pltpu.SMEM((1,), jnp.int32),
        ]

    work = lambda keys: dict(flops=2 * n * keys * 512, exps=n * keys, nbytes=4 * n * 96)
    q, start, top, part = call(
        first_kernel,
        (q_shape, m_shape, m_shape, o_shape),
        [("v", q_own), ("v", swapped), ("v", kv_own)],
        scratch(n),
        **work(n),
    )
    tops, parts = [top], [part]
    for chunks in groups[:-1]:
        keys = sum(t.shape[1] for t in chunks)
        top, part = call(
            functools.partial(next_kernel, len(chunks)),
            (m_shape, o_shape),
            [("v", t) for t in chunks] + [("v", q), ("v", start)],
            scratch(keys),
            **work(keys),
        )
        tops.append(top)
        parts.append(part)
    final = scratch(n)
    half_shape = sds((HEAD_DIM, band), BF)
    attended, partner = call(
        functools.partial(last_kernel, 2, len(tops)),
        (half_shape, half_shape),
        [("s", slot_col)] + [("v", t) for t in (*groups[-1], q, start, *tops, *parts)],
        [final[0], pltpu.VMEM((8, n), F32), pltpu.VMEM((96, n), F32), *final[1:]],
        **work(n),
    )
    attended = jnp.concatenate([attended, send(partner, swap)], axis=0)
    pieces, _ = spread(attended, "x", mirror_x, 0)
    where = [
        ("s", slot_col),
        ("s", jnp.stack([c, x, zh]).astype(jnp.int32)),
        ("v", out_weight),
    ]
    total = sds((band, model_width), F32)
    total_flops = 2 * band * model_width * model_width
    mixed = call(
        mix_first_kernel,
        total,
        where + [("v", t) for t in (*pieces[:4], *tiles)],
        flops=total_flops // 2,
        grant=10,
    )
    mixed = call(
        mix_next_kernel,
        total,
        where + [("v", t) for t in (*pieces[4:7], mixed)],
        flops=3 * total_flops // 8,
        grant=10,
        alias={6: 0},
    )
    hidden_a, hidden_b = call(
        merge_kernel,
        (sds((256, up_weight.shape[1]), BF),) * 2,
        where
        + [("v", t) for t in (*pieces[7:], mixed, gains[1])]
        + [("v", up_weight), ("v", gains[2])],
        [pltpu.VMEM((band, model_width), F32), pltpu.VMEM((4, 256, model_width), BF)],
        flops=2 * 256 * 5120 * 640 + total_flops // 8,
        grant=18,
    )
    return scatter_output(hidden_a, hidden_b, down_weight, down_bias, mirror_x)


def ring(block, rows):
    forward, backward = shift("x", 1), shift("x", -1)
    half = block.shape[1] // 2
    part = lambda k: block[k * rows : (k + 1) * rows]
    ahead, behind, far = part(1), part(3), part(2)
    from_behind = send(far[:, :half], forward)
    from_ahead = send(far[:, half:], backward)
    add = lambda p, q: (p.astype(F32) + q.astype(F32)).astype(BF)
    onward = jnp.concatenate([add(ahead[:, :half], from_behind), ahead[:, half:]], axis=1)
    back = jnp.concatenate([behind[:, :half], add(behind[:, half:], from_ahead)], axis=1)
    got_behind, got_ahead = send(onward, forward), send(back, backward)
    return part(0).astype(F32) + got_behind.astype(F32) + got_ahead.astype(F32)


def scatter_output(hidden_a, hidden_b, down_weight, down_bias, mirror):
    split = 4608
    part_b = jnp.dot(
        hidden_b, down_weight[:, split:], preferred_element_type=F32
    ).astype(BF)
    give_b, hidden_a = lax.optimization_barrier((part_b[128:], hidden_a))
    got_b = send(give_b, mirror)
    part_a = jnp.dot(
        hidden_a, down_weight[:, :split], preferred_element_type=F32
    ).astype(BF)
    total_a = ring(part_a, 64)
    got_a = send(total_a[32:].astype(BF), mirror)
    block_b = (part_b[:128].astype(F32) + got_b.astype(F32)).astype(BF)
    total_b = ring(block_b, 32)
    total_a = total_a[:32] + got_a.astype(F32)
    return (jnp.concatenate([total_a, total_b], axis=1) + down_bias[None, :]).astype(BF)


def solution(mesh):
    fine = Mesh(mesh.devices.reshape(SIZES), AXES)
    row, col = ("y", "zl", "c"), ("x", "zh")
    placed = (
        P(row, col, None),
        P(),
        P(None, col),
        P(None, col),
        P(None, col),
        P(),
        P(),
        P(None, col),
        P(col),
        P(col, None),
        P(),
    )

    return jax.shard_map(
        shards, mesh=fine, in_specs=placed, out_specs=P(row + col, None), check_vma=False
    )
```

```python
import functools
import math

import jax
import jax.numpy as jnp
import numpy as np
from jax import lax
from jax.experimental import pallas as pl
from jax.experimental.pallas import tpu as pltpu
from jax.sharding import Mesh
from jax.sharding import PartitionSpec as P


HEAD_DIM = 80
EPSILON = 1e-06
AXES = ("y", "zl", "c", "x", "zh")
SIZES = (4, 2, 2, 4, 2)
BF = jnp.bfloat16
F32 = jnp.float32
QUERY_BLOCK = 512
LIMIT = 2.0**64


def pairs(move):
    result = []
    for place in np.ndindex(*SIZES):
        there = dict(zip(AXES, place))
        there.update(move(there))
        target = tuple(there[a] % n for a, n in zip(AXES, SIZES))
        result.append(
            (int(np.ravel_multi_index(place, SIZES)), int(np.ravel_multi_index(target, SIZES)))
        )
    return result


def shift(axis, step):
    return pairs(lambda d: {axis: d[axis] + step})


def send(value, perm):
    return lax.ppermute(value, AXES, perm)


def vmem():
    return pl.BlockSpec(memory_space=pltpu.VMEM)


def smem():
    return pl.BlockSpec(memory_space=pltpu.SMEM)


def call(kernel, outs, ins, scratch=(), flops=0, nbytes=0, exps=0, grant=8, alias=None):
    specs = [smem() if k == "s" else vmem() for k, _ in ins]
    return pl.pallas_call(
        kernel,
        out_shape=outs,
        in_specs=specs,
        out_specs=jax.tree.map(lambda _: vmem(), outs),
        scratch_shapes=list(scratch),
        input_output_aliases=alias or {},
        cost_estimate=pl.CostEstimate(flops=flops, bytes_accessed=nbytes, transcendentals=exps),
        compiler_params=pltpu.CompilerParams(vmem_limit_bytes=grant * 2**20),
    )(*[a for _, a in ins])


def norm(values, gain):
    center = values - jnp.mean(values, axis=-1, keepdims=True)
    spread = jnp.mean(center * center, axis=-1, keepdims=True)
    return center * lax.rsqrt(spread + EPSILON) * gain


def project_kernel(groups, at, c_ref, gain_ref, wq, wk, wv, cos_ref, sin_ref, *refs):
    tiles = refs[: sum(groups)]
    q_out, kv_out, other_out = refs[-3:]
    mine = pl.multiple_of(c_ref[0] * HEAD_DIM, 16)
    others = pl.multiple_of((1 - c_ref[0]) * HEAD_DIM, 16)
    weight = jnp.concatenate(
        [w[pl.ds(o, HEAD_DIM), :] for o in (mine, others) for w in (wq, wk, wv)], axis=0
    )
    half = HEAD_DIM // 2
    scale = math.log2(math.e) / math.sqrt(HEAD_DIM)
    for count in groups:
        group, tiles = tiles[:count], tiles[count:]
        rows = jnp.concatenate([t[...] for t in group], axis=0).astype(F32)
        rows = norm(rows, gain_ref[...]).astype(BF)
        span = slice(at, at + rows.shape[0])
        at += rows.shape[0]
        mapped = lax.dot_general(
            weight, rows, (((1,), (1,)), ((), ())), preferred_element_type=F32
        )
        cos, sin = cos_ref[:, span], sin_ref[:, span]

        def turn(u):
            first, second = u[:half], u[half:]
            return jnp.concatenate([first * cos - second * sin, second * cos + first * sin], axis=0)

        part = [mapped[k * HEAD_DIM : (k + 1) * HEAD_DIM] for k in range(6)]
        q_out[:, span] = (turn(part[0]) * scale).astype(BF)
        kv_out[:HEAD_DIM, span] = turn(part[1]).astype(BF)
        kv_out[HEAD_DIM:, span] = part[2].astype(BF)
        other_out[:HEAD_DIM, span] = (turn(part[3]) * scale).astype(BF)
        other_out[HEAD_DIM : 2 * HEAD_DIM, span] = turn(part[4]).astype(BF)
        other_out[2 * HEAD_DIM :, span] = part[5].astype(BF)


def split_rows(m):
    hi = m.astype(BF)
    rest = m - hi.astype(F32)
    mid = rest.astype(BF)
    low = (rest - mid.astype(F32)).astype(BF)
    pad = jnp.zeros((13, m.shape[1]), BF)
    return jnp.concatenate([-hi, -mid, -low, pad], axis=0)


def attend_chunks(chunks, q_ref, m_ref, o_ref, k_all, v_all, flag):
    keys = k_all.shape[0]
    queries = q_ref.shape[1]
    step, unroll = (keys, 2) if keys <= 2048 else (keys // 2, 1)
    turns = queries // (unroll * QUERY_BLOCK)
    at = 0
    ones = jnp.ones((16, 512), BF)
    for ref in chunks:

        def place(i, carry, ref=ref, at=at):
            cols = pl.ds(pl.multiple_of(i * 512, 512), 512)
            spot = pl.ds(pl.multiple_of(at + i * 512, 512), 512)
            keys_part = ref[-2 * HEAD_DIM : -HEAD_DIM, cols]
            k_all[spot, :] = jnp.concatenate([keys_part, ones], axis=0).T
            v_all[:, spot] = jnp.concatenate([ref[-HEAD_DIM:, cols], ones], axis=0)
            return carry

        lax.fori_loop(0, ref.shape[1] // 512, place, 0)
        at += ref.shape[1]
    flag[0] = 1

    def attempt(tries, carry):
        @pl.when(flag[0] == 1)
        def _():
            o_ref[...] = jnp.zeros_like(o_ref)

            def block(t, carry):
                rows = pl.ds(pl.multiple_of((t // turns) * step, step), step)
                for i in range(unroll):
                    col = (t % turns) * (unroll * QUERY_BLOCK) + i * QUERY_BLOCK
                    cols = pl.ds(pl.multiple_of(col, QUERY_BLOCK), QUERY_BLOCK)
                    s = jnp.dot(k_all[rows, :], q_ref[:, cols], preferred_element_type=F32)
                    p = jnp.exp2(s).astype(BF)
                    o_ref[:, cols] += jnp.dot(v_all[:, rows], p, preferred_element_type=F32)
                return carry

            lax.fori_loop(0, keys // step * turns, block, 0)
            mass = o_ref[HEAD_DIM : HEAD_DIM + 8, :]
            bad = jnp.max(jnp.where(mass < LIMIT, 0.0, 1.0)) > 0.0
            flag[0] = jnp.where(jnp.logical_and(bad, tries == 0), 1, 0)

            @pl.when(flag[0] == 1)
            def _():
                m_ref[1:2, :] = jnp.zeros((1, queries), F32)

                def top_block(t, carry):
                    rows = pl.ds(pl.multiple_of((t // 8) * 512, 512), 512)
                    cols = pl.ds(pl.multiple_of((t % 8) * 256, 256), 256)
                    s = jnp.dot(k_all[rows, :], q_ref[:, cols], preferred_element_type=F32)
                    m_ref[1:2, cols] = jnp.maximum(
                        m_ref[1:2, cols], jnp.max(s, axis=0, keepdims=True)
                    )
                    return carry

                lax.fori_loop(0, keys // 512 * (queries // 256), top_block, 0)
                fresh = m_ref[0:1, :] + m_ref[1:2, :]
                m_ref[0:1, :] = fresh
                q_ref[HEAD_DIM:, :] = split_rows(fresh)

        return carry

    lax.fori_loop(0, 2, attempt, 0)


def first_kernel(own_q, swapped, kv_ref, q_out, start_out, m_ref, o_ref, q_ref, k_all, v_all, flag):
    n = own_q.shape[1]
    q_ref[:HEAD_DIM, :n] = own_q[...]
    q_ref[:HEAD_DIM, n:] = swapped[:HEAD_DIM, :]
    some = kv_ref[:HEAD_DIM, :256].T

    def start(i, carry):
        cols = pl.ds(pl.multiple_of(i * QUERY_BLOCK, QUERY_BLOCK), QUERY_BLOCK)
        s = jnp.dot(some, q_ref[:HEAD_DIM, cols], preferred_element_type=F32)
        m_ref[:, cols] = jnp.broadcast_to(jnp.max(s, axis=0, keepdims=True), (8, QUERY_BLOCK))
        return carry

    lax.fori_loop(0, 2 * n // QUERY_BLOCK, start, 0)
    q_ref[HEAD_DIM:, :] = split_rows(m_ref[0:1, :])
    q_out[...] = q_ref[...]
    start_out[...] = m_ref[...]
    attend_chunks([kv_ref, swapped], q_ref, m_ref, o_ref, k_all, v_all, flag)


def next_kernel(count, *refs):
    chunks, rest = refs[:count], refs[count:]
    q_in, m_in, m_ref, o_ref, q_ref, k_all, v_all, flag = rest
    q_ref[...] = q_in[...]
    m_ref[...] = m_in[...]
    attend_chunks(chunks, q_ref, m_ref, o_ref, k_all, v_all, flag)


def last_kernel(count, done, place, *refs):
    chunks, rest = refs[:count], refs[count:]
    q_in, m_in = rest[:2]
    tops, sums = rest[2 : 2 + done], rest[2 + done : 2 + 2 * done]
    own_ref, swap_ref, q_ref, m_ref, o_ref, k_all, v_all, flag = rest[2 + 2 * done :]
    q_ref[...] = q_in[...]
    m_ref[...] = m_in[...]
    attend_chunks(chunks, q_ref, m_ref, o_ref, k_all, v_all, flag)
    half = o_ref.shape[1] // 2
    for out_ref, lower in ((own_ref, 0), (swap_ref, half)):

        def block(turn, carry, out_ref=out_ref, lower=lower):
            for k in range(4):
                slot = turn * 4 + k
                cols = pl.ds(pl.multiple_of(lower + slot * 128, 128), 128)
                own_top = m_ref[0:1, cols]
                top = own_top
                for t in tops:
                    top = jnp.maximum(top, t[0:1, cols])
                total = o_ref[:, cols] * jnp.exp2(own_top - top)
                for t, o in zip(tops, sums):
                    total = total + o[:, cols] * jnp.exp2(t[0:1, cols] - top)
                target = pl.ds(pl.multiple_of(place[slot] * 128, 128), 128)
                mass = total[HEAD_DIM : HEAD_DIM + 1]
                out_ref[:, target] = (total[:HEAD_DIM] / mass).astype(BF)
            return carry

        lax.fori_loop(0, half // 512, block, 0)


def add_heads(slots, pieces, col_ref, c, weight_ref, base_ref, out_ref, rows_at_once=256):
    rows = []
    for slot in slots:
        for head in (c, 1 - c):
            spot = pl.multiple_of(col_ref[slot] * 160 + head * 80, 16)
            rows.append(weight_ref[pl.ds(spot, 80), :])
    weight = jnp.concatenate(rows, axis=0)

    def block(i, carry):
        spot = pl.ds(pl.multiple_of(i * rows_at_once, rows_at_once), rows_at_once)
        lhs = jnp.concatenate([p[:, spot] for p in pieces], axis=0).T
        out_ref[spot, :] = base_ref[spot, :] + jnp.dot(lhs, weight, preferred_element_type=F32)
        return carry

    lax.fori_loop(0, out_ref.shape[0] // rows_at_once, block, 0)


def mix_first_kernel(col_ref, place_ref, weight_ref, *refs):
    pieces, tiles, out_ref = refs[:4], refs[4:13], refs[13]
    starts = [col_ref[slot] * 128 for slot in range(8)] + [col_ref[7] * 128 + 64]
    for tile, start in zip(tiles, starts):

        def copy(i, carry, tile=tile, start=start):
            rows = pl.ds(pl.multiple_of(i * 32, 32), 32)
            spot = pl.ds(pl.multiple_of(start + i * 32, 32), 32)
            out_ref[spot, :] = tile[rows, :].astype(F32)
            return carry

        lax.fori_loop(0, tile.shape[0] // 32, copy, 0)
    add_heads((0, 1, 2, 3), pieces, col_ref, place_ref[0], weight_ref, out_ref, out_ref)


def mix_next_kernel(col_ref, place_ref, weight_ref, *refs):
    pieces, base_ref, out_ref = refs[:3], refs[3], refs[4]
    add_heads((4, 5, 6), pieces, col_ref, place_ref[0], weight_ref, base_ref, out_ref)


def merge_kernel(col_ref, place_ref, out_weight, *refs):
    pieces, rest = refs[:2], refs[2:]
    base_ref, gain_ref, up_weight, bias_ref, hidden_a, hidden_b, mixed_all, merged = rest
    c, x, zh = place_ref[0], place_ref[1], place_ref[2]
    width = out_weight.shape[1]
    add_heads((7,), pieces, col_ref, c, out_weight, base_ref, mixed_all, 512)
    r = lax.broadcasted_iota(jnp.int32, (128, 128), 0)
    t = lax.broadcasted_iota(jnp.int32, (128, 128), 1)
    a, b, u, w = r >> 6, (r >> 5) & 1, (r >> 3) & 3, r & 7
    pick = ((2 * u + a) * 16 + 2 * w + b == t).astype(BF)

    def settle(turn, carry):
        for k in range(4):
            s = turn * 4 + k
            spot = pl.ds(pl.multiple_of(col_ref[s] * 128, 128), 128)
            normed = norm(mixed_all[spot, :], gain_ref[...]).astype(BF)
            ordered = jnp.dot(pick, normed, preferred_element_type=F32).astype(BF)
            rows = pl.ds(pl.multiple_of(s * 32, 32), 32)
            for q in range(4):
                merged[q, rows, :] = ordered[q * 32 : (q + 1) * 32]
        return carry

    lax.fori_loop(0, 2, settle, 0)
    z = bias_ref[...]
    for q in range(4):
        z = z + jnp.dot(
            merged[q], up_weight[q * width : (q + 1) * width, :], preferred_element_type=F32
        )
    hidden = (0.5 * z * (1.0 + lax.erf(z * (1.0 / math.sqrt(2.0))))).astype(BF)
    n = hidden.shape[0]
    rows = lax.broadcasted_iota(jnp.int32, (n, n), 0)
    lane = lax.broadcasted_iota(jnp.int32, (1, n), 1)
    col = jnp.zeros((1, n), jnp.int32)
    for s in range(8):
        col = jnp.where((lane >> 5) == s, col_ref[s], col)
    raster = ((lane >> 3) & 3) * 64 + col * 8 + (lane & 7)
    owner = raster >> 5
    ahead = ((owner >> 1) - x) & 3
    other_half = (owner & 1) ^ zh
    place_a = ahead * 64 + other_half * 32 + (raster & 31)
    place_b = other_half * 128 + ahead * 32 + (raster & 31)
    for place, out in ((place_a, hidden_a), (place_b, hidden_b)):
        out[...] = jnp.dot(
            (rows == place).astype(BF), hidden, preferred_element_type=F32
        ).astype(BF)


def spread(own, axis, across, dim, extras=()):
    forward, backward = shift(axis, 1), shift(axis, -1)
    half = own.shape[dim] // 2
    plus, minus, mirror = send(own, forward), send(own, backward), send(own, across)
    plus, minus, mirror, extras = lax.optimization_barrier((plus, minus, mirror, extras))
    two = send(plus, forward)
    mirror_plus = send(plus, across)
    mirror_minus = send(mirror, backward)
    far_low = send(lax.slice_in_dim(mirror_plus, 0, half, axis=dim), forward)
    far_high = send(lax.slice_in_dim(two, half, 2 * half, axis=dim), across)
    return [own, plus, minus, mirror, two, mirror_plus, mirror_minus, far_low, far_high], extras


def shards(
    patches,
    norm_gain,
    query_weight,
    key_weight,
    value_weight,
    out_weight,
    merge_gain,
    up_weight,
    up_bias,
    down_weight,
    down_bias,
):
    band_height, tile_width, model_width = patches.shape
    tile = band_height * tile_width
    band = tile * 8
    y, zl, c = lax.axis_index("y"), lax.axis_index("zl"), lax.axis_index("c")
    x, zh = lax.axis_index("x"), lax.axis_index("zh")
    row_index = (y * 2 + zl) * 2 + c
    sds = jax.ShapeDtypeStruct

    slot_x = jnp.stack([x, x - 1, x + 1, x, x + 2, x - 1, x + 1, x + 2]) % 4
    slot_z = jnp.stack([zh, zh, zh, 1 - zh, zh, 1 - zh, 1 - zh, 1 - zh])
    slot_col = (slot_x * 2 + slot_z).astype(jnp.int32)
    local = np.arange(tile)
    row_coord = (row_index * band_height + jnp.tile(local // tile_width, 8)).astype(F32)
    col_coord = (
        (slot_col[:, None] * tile_width + (local % tile_width)[None, :]).astype(F32).reshape(-1)
    )
    frequency = 1.0 / 10000.0 ** (
        jnp.arange(HEAD_DIM // 4, dtype=F32) * 2.0 / (HEAD_DIM // 2)
    )
    angles = jnp.concatenate(
        [frequency[:, None] * row_coord[None, :], frequency[:, None] * col_coord[None, :]], axis=0
    )
    cos, sin = jnp.cos(angles), jnp.sin(angles)

    mirror_x = pairs(lambda d: {"zh": 1 - d["zh"]})
    tokens = patches.reshape(tile, model_width)
    gains = [v.reshape(1, -1) for v in (norm_gain, merge_gain, up_bias)]
    tiles, (cos, sin, gains) = spread(tokens, "x", mirror_x, 0, (cos, sin, gains))
    shapes = (
        sds((HEAD_DIM, band), BF),
        sds((2 * HEAD_DIM, band), BF),
        sds((3 * HEAD_DIM, band), BF),
    )
    fixed = [("s", c.reshape(1).astype(jnp.int32)), ("v", gains[0])]
    fixed += [("v", w.T) for w in (query_weight, key_weight, value_weight)]
    fixed += [("v", cos), ("v", sin)]
    mapped = ()
    for k, (groups, used) in enumerate(
        (((2, 2), tiles[:4]), ((2, 1), tiles[4:7]), ((2,), tiles[7:]))
    ):
        first = (0, 4, 7)[k]
        spot = len(fixed) + len(used)
        mapped = call(
            functools.partial(project_kernel, groups, first * tile),
            shapes,
            fixed + [("v", t) for t in used] + [("v", t) for t in mapped],
            flops=2 * tile * (4, 3, 1)[k] * model_width * 480,
            alias={spot + o: o for o in range(len(mapped))},
        )
    q_own, kv_own, other = mapped
    n = 2 * band
    swap = pairs(lambda d: {"c": 1 - d["c"]})
    mirror_y = pairs(lambda d: {"zl": 1 - d["zl"]})
    swapped = send(other, swap)
    forward, backward = shift("y", 1), shift("y", -1)
    near = [send(kv_own, p) for p in (forward, backward, mirror_y)]
    near += [send(swapped[HEAD_DIM:], p) for p in (forward, backward, mirror_y)]
    near = lax.optimization_barrier(near)
    plus = jnp.concatenate([near[0], near[3]], axis=1)
    mirror = jnp.concatenate([near[2], near[5]], axis=1)
    two, mirror_plus = send(plus, forward), send(plus, mirror_y)
    mirror_minus = send(mirror, backward)
    far = [send(mirror_plus[:, :band], forward), send(two[:, band:], mirror_y)]
    groups = (near, [two, mirror_plus, mirror_minus], far)
    q_shape, m_shape, o_shape = sds((96, n), BF), sds((8, n), F32), sds((96, n), F32)

    def scratch(keys):
        return [
            pltpu.VMEM((96, n), BF),
            pltpu.VMEM((keys, 96), BF),
            pltpu.VMEM((96, keys), BF),
            pltpu.SMEM((1,), jnp.int32),
        ]

    work = lambda keys: dict(flops=2 * n * keys * 512, exps=n * keys, nbytes=4 * n * 96)
    q, start, top, part = call(
        first_kernel,
        (q_shape, m_shape, m_shape, o_shape),
        [("v", q_own), ("v", swapped), ("v", kv_own)],
        scratch(n),
        **work(n),
    )
    tops, parts = [top], [part]
    for chunks in groups[:-1]:
        keys = sum(t.shape[1] for t in chunks)
        top, part = call(
            functools.partial(next_kernel, len(chunks)),
            (m_shape, o_shape),
            [("v", t) for t in chunks] + [("v", q), ("v", start)],
            scratch(keys),
            grant=12,
            **work(keys),
        )
        tops.append(top)
        parts.append(part)
    final = scratch(n)
    half_shape = sds((HEAD_DIM, band), BF)
    attended, partner = call(
        functools.partial(last_kernel, 2, len(tops)),
        (half_shape, half_shape),
        [("s", slot_col)] + [("v", t) for t in (*groups[-1], q, start, *tops, *parts)],
        [final[0], pltpu.VMEM((8, n), F32), pltpu.VMEM((96, n), F32), *final[1:]],
        **work(n),
    )
    attended = jnp.concatenate([attended, send(partner, swap)], axis=0)
    pieces, _ = spread(attended, "x", mirror_x, 0)
    where = [
        ("s", slot_col),
        ("s", jnp.stack([c, x, zh]).astype(jnp.int32)),
        ("v", out_weight),
    ]
    total = sds((band, model_width), F32)
    total_flops = 2 * band * model_width * model_width
    mixed = call(
        mix_first_kernel,
        total,
        where + [("v", t) for t in (*pieces[:4], *tiles)],
        flops=total_flops // 2,
        grant=10,
    )
    mixed = call(
        mix_next_kernel,
        total,
        where + [("v", t) for t in (*pieces[4:7], mixed)],
        flops=3 * total_flops // 8,
        grant=10,
        alias={6: 0},
    )
    hidden_a, hidden_b = call(
        merge_kernel,
        (sds((256, up_weight.shape[1]), BF),) * 2,
        where
        + [("v", t) for t in (*pieces[7:], mixed, gains[1])]
        + [("v", up_weight), ("v", gains[2])],
        [pltpu.VMEM((band, model_width), F32), pltpu.VMEM((4, 256, model_width), BF)],
        flops=2 * 256 * 5120 * 640 + total_flops // 8,
        grant=18,
    )
    return scatter_output(hidden_a, hidden_b, down_weight, down_bias, mirror_x)


def ring(block, rows, early):
    forward, backward = shift("x", 1), shift("x", -1)
    half = block.shape[1] // 2
    part = lambda k: block[k * rows : (k + 1) * rows]
    ahead, behind, far = part(1), part(3), part(2)
    add = lambda p, q: (p.astype(F32) + q.astype(F32)).astype(BF)
    from_behind = send(far[:, :half], forward)
    from_ahead = send(far[:, half:], backward)
    if early:
        high_behind = send(ahead[:, half:], forward)
        low_ahead = send(behind[:, :half], backward)
        low_behind = send(add(ahead[:, :half], from_behind), forward)
        high_ahead = send(add(behind[:, half:], from_ahead), backward)
        got_behind = jnp.concatenate([low_behind, high_behind], axis=1)
        got_ahead = jnp.concatenate([low_ahead, high_ahead], axis=1)
    else:
        onward = jnp.concatenate([add(ahead[:, :half], from_behind), ahead[:, half:]], axis=1)
        back = jnp.concatenate([behind[:, :half], add(behind[:, half:], from_ahead)], axis=1)
        got_behind, got_ahead = send(onward, forward), send(back, backward)
    return part(0).astype(F32) + got_behind.astype(F32) + got_ahead.astype(F32)


def scatter_output(hidden_a, hidden_b, down_weight, down_bias, mirror):
    split = 4864
    part_b = jnp.dot(
        hidden_b, down_weight[:, split:], preferred_element_type=F32
    ).astype(BF)
    give_b, hidden_a = lax.optimization_barrier((part_b[128:], hidden_a))
    got_b = send(give_b, mirror)
    part_a = jnp.dot(
        hidden_a, down_weight[:, :split], preferred_element_type=F32
    ).astype(BF)
    total_a = ring(part_a, 64, True)
    got_a = send(total_a[32:].astype(BF), mirror)
    block_b = (part_b[:128].astype(F32) + got_b.astype(F32)).astype(BF)
    total_b = ring(block_b, 32, True)
    total_a = total_a[:32] + got_a.astype(F32)
    return (jnp.concatenate([total_a, total_b], axis=1) + down_bias[None, :]).astype(BF)


def solution(mesh):
    fine = Mesh(mesh.devices.reshape(SIZES), AXES)
    row, col = ("y", "zl", "c"), ("x", "zh")
    placed = (
        P(row, col, None),
        P(),
        P(None, col),
        P(None, col),
        P(None, col),
        P(),
        P(),
        P(None, col),
        P(col),
        P(col, None),
        P(),
    )

    return jax.shard_map(
        shards, mesh=fine, in_specs=placed, out_specs=P(row + col, None), check_vma=False
    )
```

```python
import functools
import math

import jax
import jax.numpy as jnp
import numpy as np
from jax import lax
from jax.experimental import pallas as pl
from jax.experimental.pallas import tpu as pltpu
from jax.sharding import Mesh
from jax.sharding import PartitionSpec as P


HEAD_DIM = 80
EPSILON = 1e-06
AXES = ("y", "zl", "c", "x", "zh")
SIZES = (4, 2, 2, 4, 2)
BF = jnp.bfloat16
F32 = jnp.float32
QUERY_BLOCK = 512
LIMIT = 2.0**64


def pairs(move):
    result = []
    for place in np.ndindex(*SIZES):
        there = dict(zip(AXES, place))
        there.update(move(there))
        target = tuple(there[a] % n for a, n in zip(AXES, SIZES))
        result.append(
            (int(np.ravel_multi_index(place, SIZES)), int(np.ravel_multi_index(target, SIZES)))
        )
    return result


def shift(axis, step):
    return pairs(lambda d: {axis: d[axis] + step})


def send(value, perm):
    return lax.ppermute(value, AXES, perm)


def vmem():
    return pl.BlockSpec(memory_space=pltpu.VMEM)


def smem():
    return pl.BlockSpec(memory_space=pltpu.SMEM)


def call(kernel, outs, ins, scratch=(), flops=0, nbytes=0, exps=0, grant=8, alias=None):
    specs = [smem() if k == "s" else vmem() for k, _ in ins]
    return pl.pallas_call(
        kernel,
        out_shape=outs,
        in_specs=specs,
        out_specs=jax.tree.map(lambda _: vmem(), outs),
        scratch_shapes=list(scratch),
        input_output_aliases=alias or {},
        cost_estimate=pl.CostEstimate(flops=flops, bytes_accessed=nbytes, transcendentals=exps),
        compiler_params=pltpu.CompilerParams(vmem_limit_bytes=grant * 2**20),
    )(*[a for _, a in ins])


def norm(values, gain):
    center = values - jnp.mean(values, axis=-1, keepdims=True)
    spread = jnp.mean(center * center, axis=-1, keepdims=True)
    return center * lax.rsqrt(spread + EPSILON) * gain


def project_kernel(groups, at, c_ref, gain_ref, wq, wk, wv, cos_ref, sin_ref, *refs):
    tiles = refs[: sum(groups)]
    q_out, kv_out, other_out = refs[-3:]
    mine = pl.multiple_of(c_ref[0] * HEAD_DIM, 16)
    others = pl.multiple_of((1 - c_ref[0]) * HEAD_DIM, 16)
    weight = jnp.concatenate(
        [w[pl.ds(o, HEAD_DIM), :] for o in (mine, others) for w in (wq, wk, wv)], axis=0
    )
    half = HEAD_DIM // 2
    scale = math.log2(math.e) / math.sqrt(HEAD_DIM)
    for count in groups:
        group, tiles = tiles[:count], tiles[count:]
        rows = jnp.concatenate([t[...] for t in group], axis=0).astype(F32)
        rows = norm(rows, gain_ref[...]).astype(BF)
        span = slice(at, at + rows.shape[0])
        at += rows.shape[0]
        mapped = lax.dot_general(
            weight, rows, (((1,), (1,)), ((), ())), preferred_element_type=F32
        )
        cos, sin = cos_ref[:, span], sin_ref[:, span]

        def turn(u):
            first, second = u[:half], u[half:]
            return jnp.concatenate([first * cos - second * sin, second * cos + first * sin], axis=0)

        part = [mapped[k * HEAD_DIM : (k + 1) * HEAD_DIM] for k in range(6)]
        q_out[:, span] = (turn(part[0]) * scale).astype(BF)
        kv_out[:HEAD_DIM, span] = turn(part[1]).astype(BF)
        kv_out[HEAD_DIM:, span] = part[2].astype(BF)
        other_out[:HEAD_DIM, span] = (turn(part[3]) * scale).astype(BF)
        other_out[HEAD_DIM : 2 * HEAD_DIM, span] = turn(part[4]).astype(BF)
        other_out[2 * HEAD_DIM :, span] = part[5].astype(BF)


def split_rows(m):
    hi = m.astype(BF)
    rest = m - hi.astype(F32)
    mid = rest.astype(BF)
    low = (rest - mid.astype(F32)).astype(BF)
    pad = jnp.zeros((13, m.shape[1]), BF)
    return jnp.concatenate([-hi, -mid, -low, pad], axis=0)


def attend_chunks(chunks, q_ref, m_ref, o_ref, k_all, v_all, flag):
    keys = k_all.shape[0]
    queries = q_ref.shape[1]
    step = keys if keys <= 2048 else max(d for d in (1536, 1024) if keys % d == 0)
    turns = queries // (2 * QUERY_BLOCK)
    at = 0
    for ref in chunks:
        n = ref.shape[1]
        ones = jnp.ones((16, n), BF)
        k_all[at : at + n, :] = jnp.concatenate([ref[-2 * HEAD_DIM : -HEAD_DIM, :], ones], axis=0).T
        v_all[:, at : at + n] = jnp.concatenate([ref[-HEAD_DIM:, :], ones], axis=0)
        at += n
    flag[0] = 1

    def attempt(tries, carry):
        @pl.when(flag[0] == 1)
        def _():
            o_ref[...] = jnp.zeros_like(o_ref)

            def block(t, carry):
                rows = pl.ds(pl.multiple_of((t // turns) * step, step), step)
                for i in range(2):
                    col = (t % turns) * (2 * QUERY_BLOCK) + i * QUERY_BLOCK
                    cols = pl.ds(pl.multiple_of(col, QUERY_BLOCK), QUERY_BLOCK)
                    s = jnp.dot(k_all[rows, :], q_ref[:, cols], preferred_element_type=F32)
                    p = jnp.exp2(s).astype(BF)
                    o_ref[:, cols] += jnp.dot(v_all[:, rows], p, preferred_element_type=F32)
                return carry

            lax.fori_loop(0, keys // step * turns, block, 0)
            mass = o_ref[HEAD_DIM : HEAD_DIM + 8, :]
            bad = jnp.max(jnp.where(mass < LIMIT, 0.0, 1.0)) > 0.0
            flag[0] = jnp.where(jnp.logical_and(bad, tries == 0), 1, 0)

            @pl.when(flag[0] == 1)
            def _():
                m_ref[1:2, :] = jnp.zeros((1, queries), F32)

                def top_block(t, carry):
                    rows = pl.ds(pl.multiple_of((t // 8) * 512, 512), 512)
                    cols = pl.ds(pl.multiple_of((t % 8) * 256, 256), 256)
                    s = jnp.dot(k_all[rows, :], q_ref[:, cols], preferred_element_type=F32)
                    m_ref[1:2, cols] = jnp.maximum(
                        m_ref[1:2, cols], jnp.max(s, axis=0, keepdims=True)
                    )
                    return carry

                lax.fori_loop(0, keys // 512 * (queries // 256), top_block, 0)
                fresh = m_ref[0:1, :] + m_ref[1:2, :]
                m_ref[0:1, :] = fresh
                q_ref[HEAD_DIM:, :] = split_rows(fresh)

        return carry

    lax.fori_loop(0, 2, attempt, 0)


def first_kernel(own_q, swapped, kv_ref, q_out, start_out, m_ref, o_ref, q_ref, k_all, v_all, flag):
    n = own_q.shape[1]
    q_ref[:HEAD_DIM, :n] = own_q[...]
    q_ref[:HEAD_DIM, n:] = swapped[:HEAD_DIM, :]
    some = kv_ref[:HEAD_DIM, :256].T

    def start(i, carry):
        cols = pl.ds(pl.multiple_of(i * QUERY_BLOCK, QUERY_BLOCK), QUERY_BLOCK)
        s = jnp.dot(some, q_ref[:HEAD_DIM, cols], preferred_element_type=F32)
        m_ref[:, cols] = jnp.broadcast_to(jnp.max(s, axis=0, keepdims=True), (8, QUERY_BLOCK))
        return carry

    lax.fori_loop(0, 2 * n // QUERY_BLOCK, start, 0)
    q_ref[HEAD_DIM:, :] = split_rows(m_ref[0:1, :])
    q_out[...] = q_ref[...]
    start_out[...] = m_ref[...]
    attend_chunks([kv_ref, swapped], q_ref, m_ref, o_ref, k_all, v_all, flag)


def next_kernel(count, *refs):
    chunks, rest = refs[:count], refs[count:]
    q_in, m_in, m_ref, o_ref, q_ref, k_all, v_all, flag = rest
    q_ref[...] = q_in[...]
    m_ref[...] = m_in[...]
    attend_chunks(chunks, q_ref, m_ref, o_ref, k_all, v_all, flag)


def last_kernel(count, done, place, *refs):
    chunks, rest = refs[:count], refs[count:]
    q_in, m_in = rest[:2]
    tops, sums = rest[2 : 2 + done], rest[2 + done : 2 + 2 * done]
    own_ref, swap_ref, q_ref, m_ref, o_ref, k_all, v_all, flag = rest[2 + 2 * done :]
    q_ref[...] = q_in[...]
    m_ref[...] = m_in[...]
    attend_chunks(chunks, q_ref, m_ref, o_ref, k_all, v_all, flag)
    half = o_ref.shape[1] // 2
    for out_ref, lower in ((own_ref, 0), (swap_ref, half)):

        def block(turn, carry, out_ref=out_ref, lower=lower):
            for k in range(4):
                slot = turn * 4 + k
                cols = pl.ds(pl.multiple_of(lower + slot * 128, 128), 128)
                own_top = m_ref[0:1, cols]
                top = own_top
                for t in tops:
                    top = jnp.maximum(top, t[0:1, cols])
                total = o_ref[:, cols] * jnp.exp2(own_top - top)
                for t, o in zip(tops, sums):
                    total = total + o[:, cols] * jnp.exp2(t[0:1, cols] - top)
                target = pl.ds(pl.multiple_of(place[slot] * 128, 128), 128)
                mass = total[HEAD_DIM : HEAD_DIM + 1]
                out_ref[:, target] = (total[:HEAD_DIM] / mass).astype(BF)
            return carry

        lax.fori_loop(0, half // 512, block, 0)


def add_heads(slots, pieces, col_ref, c, weight_ref, base_ref, out_ref, rows_at_once=256):
    rows = []
    for slot in slots:
        for head in (c, 1 - c):
            spot = pl.multiple_of(col_ref[slot] * 160 + head * 80, 16)
            rows.append(weight_ref[pl.ds(spot, 80), :])
    weight = jnp.concatenate(rows, axis=0)

    def block(i, carry):
        spot = pl.ds(pl.multiple_of(i * rows_at_once, rows_at_once), rows_at_once)
        lhs = jnp.concatenate([p[:, spot] for p in pieces], axis=0).T
        out_ref[spot, :] = base_ref[spot, :] + jnp.dot(lhs, weight, preferred_element_type=F32)
        return carry

    lax.fori_loop(0, out_ref.shape[0] // rows_at_once, block, 0)


def mix_first_kernel(col_ref, place_ref, weight_ref, *refs):
    pieces, tiles, out_ref = refs[:4], refs[4:13], refs[13]
    starts = [col_ref[slot] * 128 for slot in range(8)] + [col_ref[7] * 128 + 64]
    for tile, start in zip(tiles, starts):

        def copy(i, carry, tile=tile, start=start):
            rows = pl.ds(pl.multiple_of(i * 32, 32), 32)
            spot = pl.ds(pl.multiple_of(start + i * 32, 32), 32)
            out_ref[spot, :] = tile[rows, :].astype(F32)
            return carry

        lax.fori_loop(0, tile.shape[0] // 32, copy, 0)
    add_heads((0, 1, 2, 3), pieces, col_ref, place_ref[0], weight_ref, out_ref, out_ref)


def mix_next_kernel(col_ref, place_ref, weight_ref, *refs):
    pieces, base_ref, out_ref = refs[:3], refs[3], refs[4]
    add_heads((4, 5, 6), pieces, col_ref, place_ref[0], weight_ref, base_ref, out_ref)


def merge_kernel(col_ref, place_ref, out_weight, *refs):
    pieces, rest = refs[:2], refs[2:]
    base_ref, gain_ref, up_weight, bias_ref, hidden_a, hidden_b, mixed_all, merged = rest
    c, x, zh = place_ref[0], place_ref[1], place_ref[2]
    width = out_weight.shape[1]
    add_heads((7,), pieces, col_ref, c, out_weight, base_ref, mixed_all, 512)
    r = lax.broadcasted_iota(jnp.int32, (128, 128), 0)
    t = lax.broadcasted_iota(jnp.int32, (128, 128), 1)
    a, b, u, w = r >> 6, (r >> 5) & 1, (r >> 3) & 3, r & 7
    pick = ((2 * u + a) * 16 + 2 * w + b == t).astype(BF)

    def settle(turn, carry):
        for k in range(4):
            s = turn * 4 + k
            spot = pl.ds(pl.multiple_of(col_ref[s] * 128, 128), 128)
            normed = norm(mixed_all[spot, :], gain_ref[...]).astype(BF)
            ordered = jnp.dot(pick, normed, preferred_element_type=F32).astype(BF)
            rows = pl.ds(pl.multiple_of(s * 32, 32), 32)
            for q in range(4):
                merged[q, rows, :] = ordered[q * 32 : (q + 1) * 32]
        return carry

    lax.fori_loop(0, 2, settle, 0)
    z = bias_ref[...]
    for q in range(4):
        z = z + jnp.dot(
            merged[q], up_weight[q * width : (q + 1) * width, :], preferred_element_type=F32
        )
    hidden = (0.5 * z * (1.0 + lax.erf(z * (1.0 / math.sqrt(2.0))))).astype(BF)
    n = hidden.shape[0]
    rows = lax.broadcasted_iota(jnp.int32, (n, n), 0)
    lane = lax.broadcasted_iota(jnp.int32, (1, n), 1)
    col = jnp.zeros((1, n), jnp.int32)
    for s in range(8):
        col = jnp.where((lane >> 5) == s, col_ref[s], col)
    raster = ((lane >> 3) & 3) * 64 + col * 8 + (lane & 7)
    owner = raster >> 5
    ahead = ((owner >> 1) - x) & 3
    other_half = (owner & 1) ^ zh
    place_a = ahead * 64 + other_half * 32 + (raster & 31)
    place_b = other_half * 128 + ahead * 32 + (raster & 31)
    for place, out in ((place_a, hidden_a), (place_b, hidden_b)):
        out[...] = jnp.dot(
            (rows == place).astype(BF), hidden, preferred_element_type=F32
        ).astype(BF)


def spread(own, axis, across, dim, extras=()):
    forward, backward = shift(axis, 1), shift(axis, -1)
    half = own.shape[dim] // 2
    plus, minus, mirror = send(own, forward), send(own, backward), send(own, across)
    plus, minus, mirror, extras = lax.optimization_barrier((plus, minus, mirror, extras))
    two = send(plus, forward)
    mirror_plus = send(plus, across)
    mirror_minus = send(mirror, backward)
    far_low = send(lax.slice_in_dim(mirror_plus, 0, half, axis=dim), forward)
    far_high = send(lax.slice_in_dim(two, half, 2 * half, axis=dim), across)
    return [own, plus, minus, mirror, two, mirror_plus, mirror_minus, far_low, far_high], extras


def shards(
    patches,
    norm_gain,
    query_weight,
    key_weight,
    value_weight,
    out_weight,
    merge_gain,
    up_weight,
    up_bias,
    down_weight,
    down_bias,
):
    band_height, tile_width, model_width = patches.shape
    tile = band_height * tile_width
    band = tile * 8
    y, zl, c = lax.axis_index("y"), lax.axis_index("zl"), lax.axis_index("c")
    x, zh = lax.axis_index("x"), lax.axis_index("zh")
    row_index = (y * 2 + zl) * 2 + c
    sds = jax.ShapeDtypeStruct

    slot_x = jnp.stack([x, x - 1, x + 1, x, x + 2, x - 1, x + 1, x + 2]) % 4
    slot_z = jnp.stack([zh, zh, zh, 1 - zh, zh, 1 - zh, 1 - zh, 1 - zh])
    slot_col = (slot_x * 2 + slot_z).astype(jnp.int32)
    local = np.arange(tile)
    row_coord = (row_index * band_height + jnp.tile(local // tile_width, 8)).astype(F32)
    col_coord = (
        (slot_col[:, None] * tile_width + (local % tile_width)[None, :]).astype(F32).reshape(-1)
    )
    frequency = 1.0 / 10000.0 ** (
        jnp.arange(HEAD_DIM // 4, dtype=F32) * 2.0 / (HEAD_DIM // 2)
    )
    angles = jnp.concatenate(
        [frequency[:, None] * row_coord[None, :], frequency[:, None] * col_coord[None, :]], axis=0
    )
    cos, sin = jnp.cos(angles), jnp.sin(angles)

    mirror_x = pairs(lambda d: {"zh": 1 - d["zh"]})
    tokens = patches.reshape(tile, model_width)
    gains = [v.reshape(1, -1) for v in (norm_gain, merge_gain, up_bias)]
    tiles, (cos, sin, gains) = spread(tokens, "x", mirror_x, 0, (cos, sin, gains))
    shapes = (
        sds((HEAD_DIM, band), BF),
        sds((2 * HEAD_DIM, band), BF),
        sds((3 * HEAD_DIM, band), BF),
    )
    fixed = [("s", c.reshape(1).astype(jnp.int32)), ("v", gains[0])]
    fixed += [("v", w.T) for w in (query_weight, key_weight, value_weight)]
    fixed += [("v", cos), ("v", sin)]
    mapped = ()
    for k, (groups, used) in enumerate(
        (((2, 2), tiles[:4]), ((2, 1), tiles[4:7]), ((2,), tiles[7:]))
    ):
        first = (0, 4, 7)[k]
        spot = len(fixed) + len(used)
        mapped = call(
            functools.partial(project_kernel, groups, first * tile),
            shapes,
            fixed + [("v", t) for t in used] + [("v", t) for t in mapped],
            flops=2 * tile * (4, 3, 1)[k] * model_width * 480,
            alias={spot + o: o for o in range(len(mapped))},
        )
    q_own, kv_own, other = mapped
    n = 2 * band
    swap = pairs(lambda d: {"c": 1 - d["c"]})
    mirror_y = pairs(lambda d: {"zl": 1 - d["zl"]})
    swapped = send(other, swap)
    forward, backward = shift("y", 1), shift("y", -1)
    near = [send(kv_own, p) for p in (forward, backward, mirror_y)]
    near += [send(swapped[HEAD_DIM:], p) for p in (forward, backward, mirror_y)]
    near = lax.optimization_barrier(near)
    plus = jnp.concatenate([near[0], near[3]], axis=1)
    mirror = jnp.concatenate([near[2], near[5]], axis=1)
    two, mirror_plus = send(plus, forward), send(plus, mirror_y)
    mirror_minus = send(mirror, backward)
    far = [send(mirror_plus[:, :band], forward), send(two[:, band:], mirror_y)]
    groups = (near, [two, mirror_plus, mirror_minus], far)
    q_shape, m_shape, o_shape = sds((96, n), BF), sds((8, n), F32), sds((96, n), F32)

    def scratch(keys):
        return [
            pltpu.VMEM((96, n), BF),
            pltpu.VMEM((keys, 96), BF),
            pltpu.VMEM((96, keys), BF),
            pltpu.SMEM((1,), jnp.int32),
        ]

    work = lambda keys: dict(flops=2 * n * keys * 512, exps=n * keys, nbytes=4 * n * 96)
    q, start, top, part = call(
        first_kernel,
        (q_shape, m_shape, m_shape, o_shape),
        [("v", q_own), ("v", swapped), ("v", kv_own)],
        scratch(n),
        **work(n),
    )
    tops, parts = [top], [part]
    for chunks in groups[:-1]:
        keys = sum(t.shape[1] for t in chunks)
        top, part = call(
            functools.partial(next_kernel, len(chunks)),
            (m_shape, o_shape),
            [("v", t) for t in chunks] + [("v", q), ("v", start)],
            scratch(keys),
            **work(keys),
        )
        tops.append(top)
        parts.append(part)
    final = scratch(n)
    half_shape = sds((HEAD_DIM, band), BF)
    attended, partner = call(
        functools.partial(last_kernel, 2, len(tops)),
        (half_shape, half_shape),
        [("s", slot_col)] + [("v", t) for t in (*groups[-1], q, start, *tops, *parts)],
        [final[0], pltpu.VMEM((8, n), F32), pltpu.VMEM((96, n), F32), *final[1:]],
        **work(n),
    )
    attended = jnp.concatenate([attended, send(partner, swap)], axis=0)
    pieces, _ = spread(attended, "x", mirror_x, 0)
    where = [
        ("s", slot_col),
        ("s", jnp.stack([c, x, zh]).astype(jnp.int32)),
        ("v", out_weight),
    ]
    total = sds((band, model_width), F32)
    total_flops = 2 * band * model_width * model_width
    mixed = call(
        mix_first_kernel,
        total,
        where + [("v", t) for t in (*pieces[:4], *tiles)],
        flops=total_flops // 2,
        grant=10,
    )
    mixed = call(
        mix_next_kernel,
        total,
        where + [("v", t) for t in (*pieces[4:7], mixed)],
        flops=3 * total_flops // 8,
        grant=10,
        alias={6: 0},
    )
    hidden_a, hidden_b = call(
        merge_kernel,
        (sds((256, up_weight.shape[1]), BF),) * 2,
        where
        + [("v", t) for t in (*pieces[7:], mixed, gains[1])]
        + [("v", up_weight), ("v", gains[2])],
        [pltpu.VMEM((band, model_width), F32), pltpu.VMEM((4, 256, model_width), BF)],
        flops=2 * 256 * 5120 * 640 + total_flops // 8,
        grant=18,
    )
    return scatter_output(hidden_a, hidden_b, down_weight, down_bias, mirror_x)


def ring(block, rows, early):
    forward, backward = shift("x", 1), shift("x", -1)
    half = block.shape[1] // 2
    part = lambda k: block[k * rows : (k + 1) * rows]
    ahead, behind, far = part(1), part(3), part(2)
    add = lambda p, q: (p.astype(F32) + q.astype(F32)).astype(BF)
    from_behind = send(far[:, :half], forward)
    from_ahead = send(far[:, half:], backward)
    if early:
        high_behind = send(ahead[:, half:], forward)
        low_ahead = send(behind[:, :half], backward)
        low_behind = send(add(ahead[:, :half], from_behind), forward)
        high_ahead = send(add(behind[:, half:], from_ahead), backward)
        got_behind = jnp.concatenate([low_behind, high_behind], axis=1)
        got_ahead = jnp.concatenate([low_ahead, high_ahead], axis=1)
    else:
        onward = jnp.concatenate([add(ahead[:, :half], from_behind), ahead[:, half:]], axis=1)
        back = jnp.concatenate([behind[:, :half], add(behind[:, half:], from_ahead)], axis=1)
        got_behind, got_ahead = send(onward, forward), send(back, backward)
    return part(0).astype(F32) + got_behind.astype(F32) + got_ahead.astype(F32)


def scatter_output(hidden_a, hidden_b, down_weight, down_bias, mirror):
    split = 4608
    part_b = jnp.dot(
        hidden_b, down_weight[:, split:], preferred_element_type=F32
    ).astype(BF)
    give_b, hidden_a = lax.optimization_barrier((part_b[128:], hidden_a))
    got_b = send(give_b, mirror)
    part_a = jnp.dot(
        hidden_a, down_weight[:, :split], preferred_element_type=F32
    ).astype(BF)
    total_a = ring(part_a, 64, True)
    got_a = send(total_a[32:].astype(BF), mirror)
    block_b = (part_b[:128].astype(F32) + got_b.astype(F32)).astype(BF)
    total_b = ring(block_b, 32, False)
    total_a = total_a[:32] + got_a.astype(F32)
    return (jnp.concatenate([total_a, total_b], axis=1) + down_bias[None, :]).astype(BF)


def solution(mesh):
    fine = Mesh(mesh.devices.reshape(SIZES), AXES)
    row, col = ("y", "zl", "c"), ("x", "zh")
    placed = (
        P(row, col, None),
        P(),
        P(None, col),
        P(None, col),
        P(None, col),
        P(),
        P(),
        P(None, col),
        P(col),
        P(col, None),
        P(),
    )

    return jax.shard_map(
        shards, mesh=fine, in_specs=placed, out_specs=P(row + col, None), check_vma=False
    )
```
